32 devices in a mesh: fsdp: 8 (over z, y), tp: 4 (over x, core).
Axes of the slice: x: 2, y: 2, z: 4, core: 2. Of those that a mesh axis runs over, the one named last changes fastest.
Arguments:
- layer_input: bfloat16 [8192, 768], P(('fsdp', 'tp')), may hold values from -12 to 12
- out_cotangent: bfloat16 [8192, 768], P(('fsdp', 'tp')), may hold values from -12 to 12
- segments: int32 [8, 1024], P('fsdp'), may hold values from 0 to 3, never falling along the last dimension, each value on 1 to 512 neighbouring positions
- norm_gain: float32 [768], replicated, may hold values from 0.5 to 1.5
- norm_bias: float32 [768], replicated, may hold values from -3 to 3
- qkv_weight: bfloat16 [768, 2304], P('fsdp', 'tp'), may hold values from -20 to 20
- qkv_bias: float32 [2304], P('tp'), may hold values from -3 to 3
- out_weight: bfloat16 [768, 768], P('tp', 'fsdp'), may hold values from -0.875 to 0.875
- out_bias: float32 [768], replicated, may hold values from -3 to 3
- up_weight: bfloat16 [768, 3072], P('fsdp', 'tp'), may hold values from -0.21875 to 0.21875
- up_bias: float32 [3072], P('tp'), may hold values from -3 to 3
- down_weight: bfloat16 [3072, 768], P('tp', 'fsdp'), may hold values from -0.109375 to 0.109375
- down_bias: float32 [768], replicated, may hold values from -3 to 3
Outputs:
- layer_output: bfloat16 [8192, 768], P(('fsdp', 'tp'))
- input_grad: bfloat16 [8192, 768], P(('fsdp', 'tp'))
- norm_gain_grad: float32 [768], replicated
- norm_bias_grad: float32 [768], replicated
- qkv_weight_grad: float32 [768, 2304], P('fsdp', 'tp')
- qkv_bias_grad: float32 [2304], P('tp')
- out_weight_grad: float32 [768, 768], P('tp', 'fsdp')
- out_bias_grad: float32 [768], replicated
- up_weight_grad: float32 [768, 3072], P('fsdp', 'tp')
- up_bias_grad: float32 [3072], P('tp')
- down_weight_grad: float32 [3072, 768], P('tp', 'fsdp')
- down_bias_grad: float32 [768], replicated
The draws below stay inside these ranges and needn't reach their ends.
Inputs may be any that keep to these rules, and one draw needn't show every extreme that they name: `segments`: each row is one sequence of 1024 tokens; its numbers name documents, never fall along the row, and each document spans 1 to 512 tokens, one exactly 512.
All inputs are finite; a program needn't handle non-finite values.
Results may differ from the reference program's by a relative error of at most 0.01.
Values may be sent and summed in bfloat16 or wider, within the bound.
A program may use at most 128 MiB of HBM per device.

```python
import math
import jax
import jax.numpy as jnp
import numpy as np
from jax import lax

D = 768
HEADS = 12
HEAD_DIM = 64
FF = 3072
ROT = 16
SEQ = 1024
SEQS = 8
TOKENS = 8192
DOCS = 4
MOST = 512


def draw_qkv_weight(key, part):
    drawn = jnp.clip(jax.random.normal(key, (D, HEADS, 3, HEAD_DIM), jnp.float32), -6.0, 6.0) * D ** (-0.5)
    return drawn.reshape(D, 3 * D).astype(jnp.bfloat16)


def strengthened(array, rng, source, target, blocks, factor):
    owner, partner = [(jnp.arange(array.shape[position]) // (array.shape[position] // blocks)).reshape([-1 if axis == position else 1 for axis in range(array.ndim)]) for position in (source, target)]
    chosen = jax.random.permutation(rng, blocks)[partner]
    strong = (owner == chosen) | (owner == (partner + blocks // 2) % blocks)
    return jnp.where(strong, factor * array, array)


def steps_of(rng, extent, shards, least, high):
    level = 1.0
    for dim, blocks in shards:
        heights = jax.random.uniform(jax.random.fold_in(jax.random.fold_in(rng, 6), dim), (blocks,), jnp.float32, least / len(shards), high / len(shards))
        level = level * jnp.repeat(jnp.exp(heights), extent[dim] // blocks).reshape((-1,) + (1,) * (len(extent) - 1 - dim))
    return level


def profile(number_of, total, most, lean):
    portions = [(1 << 20) // math.isqrt(grade ** lean) + 1 for grade in range(2, number_of + 1)]
    rest, holding = total - most - (number_of - 1), [1] * (number_of - 1)
    while rest > 0:
        candidates = [i for i in range(number_of - 1) if holding[i] < most]
        mass, budget = sum([portions[i] for i in candidates]), rest
        for i in candidates:
            addition = min(most - holding[i], max(1, budget * portions[i] // mass), rest)
            holding[i] = holding[i] + addition
            rest = rest - addition
    return np.array([most] + holding)


def uneven_parts(stream_key, number_of, total, bound, skew):
    if number_of == 2:
        one = jax.random.randint(stream_key, (), max(1, total - bound), min(bound, total - 1) + 1)
        return jnp.stack([one, total - one])
    tallies = jnp.asarray(profile(number_of, total, bound, skew), jnp.int32)
    couples = (number_of - 1) // 2
    giver, taker = tallies[1:1 + 2 * couples:2], tallies[2:2 + 2 * couples:2]
    margin = jnp.minimum(giver - 1, bound - taker)
    passed = jax.random.randint(jax.random.fold_in(stream_key, 1), (couples,), 0, 1 << 20) % (margin + 1)
    tallies = tallies.at[1:1 + 2 * couples:2].set(giver - passed).at[2:2 + 2 * couples:2].set(taker + passed)
    return tallies[jax.random.permutation(jax.random.fold_in(stream_key, 2), number_of)]


def normal_values(key, shape, width, reach, cuts=(), held_as=jnp.bfloat16):
    entries = jax.random.normal(key, shape, jnp.float32) * width
    if len(cuts) > 0:
        entries = steps_of(key, shape, cuts, -0.22, 0.18) * entries
    return jnp.clip(entries, min=-reach, max=reach).astype(held_as)


def noise_with(key, dims, deviation, most, pieces, heavy, kind=jnp.bfloat16):
    values = deviation * jax.random.normal(key, dims, jnp.float32)
    if pieces:
        values = values * steps_of(key, dims, pieces, -0.22, 0.18)
    return jnp.clip(strengthened(values, jax.random.fold_in(key, 3), *heavy), -most, most).astype(kind)


def setup_inputs(seed: int = 0) -> dict:
    key_list = jax.random.split(jax.random.key(seed), 14)
    layer_input = noise_with(key_list[0], (TOKENS, D), 1.0, 12.0, ((0, 32),), (0, 1, 32, 2.75))
    out_cotangent = noise_with(key_list[1], (TOKENS, D), 1.0, 12.0, ((0, 32),), (0, 1, 32, 2.75))
    segments = jax.vmap(lambda own: jnp.searchsorted(jnp.cumsum(uneven_parts(own, DOCS, SEQ, MOST, 1)), jnp.arange(SEQ), side="right"))(jax.random.split(key_list[2], SEQS)).reshape((SEQS, SEQ)).astype(jnp.int32)
    norm_gain = jnp.clip(1.0 + 0.1 * jax.random.normal(key_list[3], (D,), jnp.float32), 0.5, 1.5)
    norm_bias = normal_values(key_list[4], (D,), 0.5, 3.0, (), jnp.float32)
    qkv_weight = draw_qkv_weight(jax.random.fold_in(key_list[13], 71), 0)
    qkv_bias = normal_values(key_list[6], (3 * D,), 0.5, 3.0, ((0, 4),), jnp.float32)
    out_weight = normal_values(key_list[7], (D, D), (D // 16) ** -0.5, 0.875, ((0, 4), (1, 8)))
    out_bias = normal_values(key_list[8], (D,), 0.5, 3.0, (), jnp.float32)
    up_weight = normal_values(key_list[9], (D, FF), D ** -0.5, 0.21875, ((0, 8), (1, 4)))
    up_bias = normal_values(key_list[10], (FF,), 0.5, 3.0, ((0, 4),), jnp.float32)
    down_weight = normal_values(key_list[11], (FF, D), FF ** -0.5, 0.109375, ((0, 4), (1, 8)))
    down_bias = normal_values(key_list[12], (D,), 0.5, 3.0, (), jnp.float32)
    return dict(layer_input=layer_input, out_cotangent=out_cotangent, segments=segments, norm_gain=norm_gain, norm_bias=norm_bias, qkv_weight=qkv_weight, qkv_bias=qkv_bias, out_weight=out_weight, out_bias=out_bias, up_weight=up_weight, up_bias=up_bias, down_weight=down_weight, down_bias=down_bias)


EPSILON = 1e-05
ROTARY_BASE = 10000.0

def layer_norm(values, gain, shift):
    center = values - lax.optimization_barrier(jnp.mean(values, axis=-1, keepdims=True))
    spread = lax.optimization_barrier(jnp.mean(center * center, axis=-1, keepdims=True))
    inverse = lax.rsqrt(spread + EPSILON)
    normed = center * inverse
    return (normed, inverse, normed * gain + shift)

def gelu_value(pre_act):
    return 0.5 * pre_act * (1.0 + lax.erf(pre_act * 0.7071067811865476))

def gelu_slope(pre_act):
    return 0.5 * (1.0 + lax.erf(pre_act * 0.7071067811865476)) + pre_act * jnp.exp(-0.5 * pre_act * pre_act) * 0.3989422804014327

def positions_of(segment_row):
    length = segment_row.shape[0]
    counter = jnp.arange(length, dtype=jnp.int32)
    is_start = jnp.concatenate([jnp.ones((1,), dtype=jnp.bool_), segment_row[1:] != segment_row[:-1]])
    starts = lax.cummax(jnp.where(is_start, counter, jnp.zeros_like(counter)), axis=0)
    return counter - starts

def rotary_tables(positions):
    halves = ROT // 2
    inverse_freq = ROTARY_BASE ** (-(jnp.arange(halves, dtype=jnp.float32) * 2.0) / ROT)
    angles = positions.astype(jnp.float32)[:, None] * inverse_freq[None, :]
    cos_table = jnp.cos(angles)
    sin_table = jnp.sin(angles)
    return (jnp.concatenate([cos_table, cos_table], axis=-1), jnp.concatenate([sin_table, sin_table], axis=-1))

def rotate(tensor, cos_table, sin_table):
    halves = ROT // 2
    turned_part = tensor[..., :ROT]
    turned = jnp.concatenate([-turned_part[..., halves:], turned_part[..., :halves]], axis=-1)
    spun = turned_part * cos_table[:, None, :] + turned * sin_table[:, None, :]
    return jnp.concatenate([spun, tensor[..., ROT:]], axis=-1)

def unrotate(grad_in, cos_table, sin_table):
    halves = ROT // 2
    turned_part = grad_in[..., :ROT]
    scaled = turned_part * sin_table[:, None, :]
    back = jnp.concatenate([scaled[..., halves:], -scaled[..., :halves]], axis=-1)
    return jnp.concatenate([turned_part * cos_table[:, None, :] + back, grad_in[..., ROT:]], axis=-1)

def scores_of(queries, keys_in, allowed, score_scale):
    scores = jnp.einsum('qhd,khd->hqk', queries.astype(jnp.float32), keys_in.astype(jnp.float32)) * score_scale
    return jnp.where(allowed[None], scores, -jnp.inf)

def attend(queries, keys_in, values_in, allowed, score_scale):
    scores = scores_of(queries, keys_in, allowed, score_scale)
    highest = lax.optimization_barrier(jnp.max(scores, axis=-1, keepdims=True))
    log_total = highest + jnp.log(lax.optimization_barrier(jnp.sum(jnp.exp(scores - highest), axis=-1, keepdims=True)))
    weights = jnp.exp(scores - log_total).astype(jnp.bfloat16)
    mixed = jnp.einsum('hqk,khd->qhd', weights.astype(jnp.float32), values_in.astype(jnp.float32))
    return (mixed.astype(jnp.bfloat16), log_total)

def attend_back(queries, keys_in, values_in, mixed, grad_mixed, log_total, allowed, score_scale):
    scores = scores_of(queries, keys_in, allowed, score_scale)
    probs = jnp.exp(scores - log_total)
    weights = probs.astype(jnp.bfloat16)
    delta = lax.optimization_barrier(jnp.sum(grad_mixed.astype(jnp.float32) * mixed.astype(jnp.float32), axis=-1))
    grad_values = jnp.einsum('hqk,qhd->khd', weights.astype(jnp.float32), grad_mixed.astype(jnp.float32))
    grad_probs = jnp.einsum('qhd,khd->hqk', grad_mixed.astype(jnp.float32), values_in.astype(jnp.float32))
    grad_scores = (probs * (grad_probs - delta.T[:, :, None]) * score_scale).astype(jnp.bfloat16)
    grad_queries = jnp.einsum('hqk,khd->qhd', grad_scores.astype(jnp.float32), keys_in.astype(jnp.float32))
    grad_keys = jnp.einsum('hqk,qhd->khd', grad_scores.astype(jnp.float32), queries.astype(jnp.float32))
    return (grad_queries, grad_keys, grad_values)

def reference(layer_input, out_cotangent, segments, norm_gain, norm_bias, qkv_weight, qkv_bias, out_weight, out_bias, up_weight, up_bias, down_weight, down_bias):
    score_scale = HEAD_DIM ** (-0.5)
    inputs_seq = layer_input.reshape(SEQS, SEQ, D)
    cotan_seq = out_cotangent.reshape(SEQS, SEQ, D)

    def one_sequence(carry, member):
        input_rows, cotan_rows, segment_row = member
        own_rows = input_rows.astype(jnp.float32)
        normed, inverse, shifted = layer_norm(own_rows, norm_gain, norm_bias)
        features = shifted.astype(jnp.bfloat16)
        packed = (jnp.dot(features, qkv_weight, preferred_element_type=jnp.float32) + qkv_bias).reshape(SEQ, HEADS, 3, HEAD_DIM)
        cos_table, sin_table = rotary_tables(positions_of(segment_row))
        queries = rotate(packed[:, :, 0], cos_table, sin_table).astype(jnp.bfloat16)
        keys_all = rotate(packed[:, :, 1], cos_table, sin_table).astype(jnp.bfloat16)
        values_all = packed[:, :, 2].astype(jnp.bfloat16)
        counter = jnp.arange(SEQ, dtype=jnp.int32)
        allowed = (segment_row[:, None] == segment_row[None, :]) & (counter[:, None] >= counter[None, :])
        mixed, log_total = attend(queries, keys_all, values_all, allowed, score_scale)
        mixed_rows = mixed.reshape(SEQ, D)
        pre_act = jnp.dot(features, up_weight, preferred_element_type=jnp.float32) + up_bias
        gelu_rows = gelu_value(pre_act).astype(jnp.bfloat16)
        branch = jnp.dot(mixed_rows, out_weight, preferred_element_type=jnp.float32) + jnp.dot(gelu_rows, down_weight, preferred_element_type=jnp.float32)
        output_rows = (own_rows + branch + out_bias + down_bias).astype(jnp.bfloat16)
        cot_rows = cotan_rows.astype(jnp.float32)
        down_grad = jnp.dot(gelu_rows.T, cotan_rows, preferred_element_type=jnp.float32)
        grad_pre = jnp.dot(cotan_rows, down_weight.T, preferred_element_type=jnp.float32) * gelu_slope(pre_act)
        pre_grads = grad_pre.astype(jnp.bfloat16)
        up_grad = jnp.dot(features.T, pre_grads, preferred_element_type=jnp.float32)
        up_bias_part = lax.optimization_barrier(jnp.sum(grad_pre, axis=0))
        feature_grad = jnp.dot(pre_grads, up_weight.T, preferred_element_type=jnp.float32)
        out_grad = jnp.dot(mixed_rows.T, cotan_rows, preferred_element_type=jnp.float32)
        mixed_grad = jnp.dot(cotan_rows, out_weight.T, preferred_element_type=jnp.float32).astype(jnp.bfloat16).reshape(SEQ, HEADS, HEAD_DIM)
        grad_q, grad_k, grad_v = attend_back(queries, keys_all, values_all, mixed, mixed_grad, log_total, allowed, score_scale)
        grad_q = unrotate(grad_q, cos_table, sin_table)
        grad_k = unrotate(grad_k, cos_table, sin_table)
        packed_grad = jnp.stack([grad_q, grad_k, grad_v], axis=2).reshape(SEQ, 3 * D)
        qkv_bias_part = lax.optimization_barrier(jnp.sum(packed_grad, axis=0))
        packed_bf = packed_grad.astype(jnp.bfloat16)
        qkv_grad = jnp.dot(features.T, packed_bf, preferred_element_type=jnp.float32)
        feature_grad = feature_grad + jnp.dot(packed_bf, qkv_weight.T, preferred_element_type=jnp.float32)
        gain_part = lax.optimization_barrier(jnp.sum(feature_grad * normed, axis=0))
        shift_part = lax.optimization_barrier(jnp.sum(feature_grad, axis=0))
        scaled = feature_grad * norm_gain
        input_rows_grad = cot_rows + inverse * (scaled - lax.optimization_barrier(jnp.mean(scaled, axis=-1, keepdims=True)) - normed * lax.optimization_barrier(jnp.mean(scaled * normed, axis=-1, keepdims=True)))
        bias_part = lax.optimization_barrier(jnp.sum(cot_rows, axis=0))
        parts = (gain_part, shift_part, qkv_grad, qkv_bias_part, out_grad, bias_part, up_grad, up_bias_part, down_grad)
        carry = tuple((total + piece for total, piece in zip(carry, parts)))
        return (carry, (output_rows, input_rows_grad.astype(jnp.bfloat16)))
    start_carry = (jnp.zeros((D,), jnp.float32), jnp.zeros((D,), jnp.float32), jnp.zeros((D, 3 * D), jnp.float32), jnp.zeros((3 * D,), jnp.float32), jnp.zeros((D, D), jnp.float32), jnp.zeros((D,), jnp.float32), jnp.zeros((D, FF), jnp.float32), jnp.zeros((FF,), jnp.float32), jnp.zeros((FF, D), jnp.float32))
    totals, stacked = lax.scan(one_sequence, start_carry, (inputs_seq, cotan_seq, segments))
    layer_output = stacked[0].reshape(TOKENS, D)
    input_grad = stacked[1].reshape(TOKENS, D)
    gain_grad, shift_grad, qkv_grad, qkv_bias_grad, out_grad, bias_grad, up_grad, up_bias_grad, down_grad = totals
    return (layer_output, input_grad, gain_grad, shift_grad, qkv_grad, qkv_bias_grad, out_grad, bias_grad, up_grad, up_bias_grad, down_grad, bias_grad)
```

```python
import functools

import jax
import jax.numpy as jnp
from jax import lax
from jax.experimental import pallas as pl
from jax.experimental.pallas import tpu as pltpu
from jax.sharding import PartitionSpec as P

HEAD_DIM = 64
ROT = 16


EPSILON = 1e-05
ROTARY_BASE = 10000.0


def layer_norm(values, gain, shift):
    center = values - jnp.mean(values, axis=-1, keepdims=True)
    spread = jnp.mean(center * center, axis=-1, keepdims=True)
    inverse = lax.rsqrt(spread + EPSILON)
    normed = center * inverse
    return (normed, inverse, normed * gain + shift)


def gelu_value(pre_act):
    return 0.5 * pre_act * (1.0 + lax.erf(pre_act * 0.7071067811865476))


def gelu_slope(pre_act):
    return (
        0.5 * (1.0 + lax.erf(pre_act * 0.7071067811865476))
        + pre_act * jnp.exp(-0.5 * pre_act * pre_act) * 0.3989422804014327
    )


def positions_of(segment_row):
    length = segment_row.shape[0]
    counter = jnp.arange(length, dtype=jnp.int32)
    is_start = jnp.concatenate(
        [jnp.ones((1,), dtype=jnp.bool_), segment_row[1:] != segment_row[:-1]]
    )
    starts = lax.cummax(jnp.where(is_start, counter, jnp.zeros_like(counter)), axis=0)
    return counter - starts


def rotary_tables(positions):
    halves = ROT // 2
    inverse_freq = ROTARY_BASE ** (-(jnp.arange(halves, dtype=jnp.float32) * 2.0) / ROT)
    angles = positions.astype(jnp.float32)[:, None] * inverse_freq[None, :]
    cos_table = jnp.cos(angles)
    sin_table = jnp.sin(angles)
    return (
        jnp.concatenate([cos_table, cos_table], axis=-1),
        jnp.concatenate([sin_table, sin_table], axis=-1),
    )


def cross_rows(left, right):
    return lax.dot_general(
        left, right, (((0,), (0,)), ((), ())), preferred_element_type=jnp.float32
    )


def cross_cols(left, right):
    return lax.dot_general(
        left, right, (((1,), (1,)), ((), ())), preferred_element_type=jnp.float32
    )


MESH = pl.DeviceIdType.MESH


def place(fsdp, tp):
    f = lax.axis_index("fsdp")
    t = lax.axis_index("tp")
    pair = lax.rem(f, 2)
    line = lax.div(f, 2)
    return f, t, pair, line


def remote(source, target, send, recv, device):
    return pltpu.make_async_remote_copy(
        src_ref=source,
        dst_ref=target,
        send_sem=send,
        recv_sem=recv,
        device_id=device,
        device_id_type=MESH,
    )


def each(first, last, action):
    def step_of(step, carry):
        action(step)
        return carry

    lax.fori_loop(first, last, step_of, 0)


def greet(fsdp, tp):
    f, t, _, _ = place(fsdp, tp)
    barrier = pltpu.get_barrier_semaphore()
    each(
        1,
        fsdp,
        lambda step: pl.semaphore_signal(
            barrier, inc=1, device_id=(lax.rem(f + step, fsdp), t), device_id_type=MESH
        ),
    )
    each(
        1,
        tp,
        lambda step: pl.semaphore_signal(
            barrier, inc=1, device_id=(f, lax.rem(t + step, tp)), device_id_type=MESH
        ),
    )
    pl.semaphore_wait(barrier, fsdp + tp - 2)


def gather_kernel(
    fsdp, tp, w_ref, h_ref, c_ref, w_out, h_out, c_out, w_send, w_recv, p_send, p_recv, r_send, r_recv
):
    f, t, pair, line = place(fsdp, tp)
    lines = fsdp // 2
    greet(fsdp, tp)
    partner = 2 * line + 1 - pair

    def along(step, slot):
        other = lax.rem(line + step, lines)
        return remote(
            w_ref, w_out.at[slot], w_send.at[step], w_recv.at[step], (2 * other + pair, t)
        )

    def across(step, source, slot):
        return remote(source, w_out.at[slot], p_send.at[step], p_recv.at[step], (partner, t))

    def beside(step, which, source, target, slot):
        return remote(
            source,
            target.at[slot],
            r_send.at[which, step],
            r_recv.at[which, step],
            (f, lax.rem(t + step, tp)),
        )

    def came(step, side):
        return 2 * lax.rem(line + lines - step, lines) + side

    across(0, w_ref, f).start()
    each(1, lines, lambda step: along(step, f).start())
    each(1, tp, lambda step: beside(step, 0, h_ref, h_out, t).start())
    each(1, tp, lambda step: beside(step, 1, c_ref, c_out, t).start())
    w_out[f] = w_ref[...]
    h_out[t] = h_ref[...]
    c_out[t] = c_ref[...]

    def forward(step):
        slot = came(step, pair)
        along(step, slot).wait_recv()
        across(step, w_out.at[slot], slot).start()

    each(1, lines, forward)

    def settle(step):
        slot = lax.rem(t + tp - step, tp)
        beside(step, 0, h_ref, h_out, slot).wait()
        beside(step, 1, c_ref, c_out, slot).wait()

    each(1, tp, settle)
    each(1, lines, lambda step: along(step, f).wait_send())

    def finish(step):
        across(step, w_ref, came(step, 1 - pair)).wait()

    each(0, lines, finish)


def gather_all(weights, features, cotangent):
    fsdp = lax.axis_size("fsdp")
    tp = lax.axis_size("tp")
    vmem = pl.BlockSpec(memory_space=pltpu.VMEM)
    shapes = (
        jax.ShapeDtypeStruct((fsdp,) + weights.shape, weights.dtype),
        jax.ShapeDtypeStruct((tp,) + features.shape, features.dtype),
        jax.ShapeDtypeStruct((tp,) + cotangent.shape, cotangent.dtype),
    )
    dma = pltpu.SemaphoreType.DMA
    w_all, h_all, c_all = pl.pallas_call(
        functools.partial(gather_kernel, fsdp, tp),
        out_shape=shapes,
        in_specs=[vmem] * 3,
        out_specs=(vmem,) * 3,
        scratch_shapes=[
            dma((fsdp // 2,)),
            dma((fsdp // 2,)),
            dma((fsdp // 2,)),
            dma((fsdp // 2,)),
            dma((2, tp)),
            dma((2, tp)),
        ],
        compiler_params=pltpu.CompilerParams(
            collective_id=1, has_side_effects=True, vmem_limit_bytes=48 * 1024 * 1024
        ),
        name="gather_all",
    )(weights, features, cotangent)
    return (
        w_all.reshape(fsdp * weights.shape[0], weights.shape[1]),
        h_all.reshape(tp * features.shape[0], features.shape[1]),
        c_all.reshape(tp * cotangent.shape[0], cotangent.shape[1]),
    )


def scatter_kernel(
    fsdp,
    tp,
    many,
    *refs,
):
    g_refs, refs = refs[:many], refs[many:]
    b_ref, d_ref, n_ref, v_ref = refs[:4]
    g_outs, refs = refs[4 : 4 + many], refs[4 + many :]
    b_out, d_out, v_out = refs[:3]
    halves, joined, lands = (refs[3 + many * i : 3 + many * (i + 1)] for i in range(3))
    (
        b_land,
        d_land,
        rows,
        first,
        second,
        p_send,
        p_recv,
        w_send,
        w_recv,
        r_send,
        r_recv,
        v_send,
        v_recv,
        u_send,
        u_recv,
    ) = refs[3 + 3 * many :]
    f, t, pair, line = place(fsdp, tp)
    lines = fsdp // 2
    greet(fsdp, tp)
    partner = 2 * line + 1 - pair

    def ahead(step):
        return lax.rem(line + step, lines)

    def across(i, step):
        return remote(
            g_refs[i].at[2 * ahead(step) + 1 - pair],
            halves[i].at[step],
            p_send.at[i, step],
            p_recv.at[i, step],
            (partner, t),
        )

    def along(i, step):
        return remote(
            joined[i].at[step],
            lands[i].at[step],
            w_send.at[i, step],
            w_recv.at[i, step],
            (2 * ahead(step) + pair, t),
        )

    def beside(step, which, source, target):
        return remote(
            source.at[lax.rem(t + step, tp)],
            target.at[step],
            r_send.at[which, step],
            r_recv.at[which, step],
            (f, lax.rem(t + step, tp)),
        )

    def start_beside(step):
        beside(step, 1, d_ref, d_land).start()
        beside(step, 0, b_ref, b_land).start()

    def start_across(step):
        for i in range(many):
            across(i, step).start()

    each(1, lines, start_across)
    start_across(0)
    each(1, tp, start_beside)

    def join(step):
        for i in range(many):
            across(i, step).wait_recv()
            joined[i][step] = (
                g_refs[i][2 * ahead(step) + pair].astype(jnp.float32)
                + halves[i][step].astype(jnp.float32)
            ).astype(joined[i].dtype)
            along(i, step).start()

    each(1, lines, join)
    for i in range(many):
        across(i, 0).wait_recv()
        g_outs[i][...] = g_refs[i][f].astype(jnp.float32) + halves[i][0].astype(jnp.float32)

    d_out[...] = d_ref[t].astype(jnp.float32)
    b_out[...] = b_ref[t].astype(jnp.float32)

    def gather_d(step):
        beside(step, 1, d_ref, d_land).wait()
        d_out[...] += d_land[step].astype(jnp.float32)

    def gather_b(step):
        beside(step, 0, b_ref, b_land).wait()
        b_out[...] += b_land[step].astype(jnp.float32)

    each(1, tp, gather_d)
    rows[...] = v_ref[...]
    rows[0:1] = jnp.sum(d_out[...] * n_ref[...], axis=0, keepdims=True)
    rows[1:2] = jnp.sum(d_out[...], axis=0, keepdims=True)

    def spread(step, slot):
        return remote(
            rows,
            first.at[slot],
            v_send.at[step],
            v_recv.at[step],
            (lax.rem(f + step, fsdp), t),
        )

    each(1, fsdp, lambda step: spread(step, f).start())
    first[f] = rows[...]
    each(1, tp, gather_b)

    def collect(step):
        for i in range(many):
            along(i, step).wait_recv()
            g_outs[i][...] += lands[i][step].astype(jnp.float32)

    each(1, lines, collect)
    each(1, fsdp, lambda step: spread(step, lax.rem(f + fsdp - step, fsdp)).wait())
    total = lax.fori_loop(1, fsdp, lambda step, value: value + first[step], first[0])
    second[t] = total[:8]
    v_out[...] = total

    def share(step, slot):
        return remote(
            second.at[t],
            second.at[slot],
            u_send.at[step],
            u_recv.at[step],
            (f, lax.rem(t + step, tp)),
        )

    each(1, tp, lambda step: share(step, t).start())

    def sent_along(step):
        for i in range(many):
            along(i, step).wait_send()

    def sent_across(step):
        for i in range(many):
            across(i, step).wait_send()

    each(1, lines, sent_along)
    each(0, lines, sent_across)
    each(1, tp, lambda step: share(step, lax.rem(t + tp - step, tp)).wait())
    whole = second[0]
    for step in range(1, tp):
        whole = whole + second[step]
    v_out[:8] = whole


def scatter_all(grads, branch, feature_grad, normed, vectors):
    fsdp = lax.axis_size("fsdp")
    tp = lax.axis_size("tp")
    lines = fsdp // 2
    grads = [grad.reshape(fsdp, -1, grad.shape[1]) for grad in grads]
    many = len(grads)
    branch = branch.reshape(tp, -1, branch.shape[1])
    feature_grad = feature_grad.reshape(tp, -1, feature_grad.shape[1])
    vmem = pl.BlockSpec(memory_space=pltpu.VMEM)
    dma = pltpu.SemaphoreType.DMA
    f32 = jnp.float32
    return pl.pallas_call(
        functools.partial(scatter_kernel, fsdp, tp, many),
        out_shape=(
            *(jax.ShapeDtypeStruct(grad.shape[1:], f32) for grad in grads),
            jax.ShapeDtypeStruct(branch.shape[1:], f32),
            jax.ShapeDtypeStruct(feature_grad.shape[1:], f32),
            jax.ShapeDtypeStruct(vectors.shape, f32),
        ),
        in_specs=[vmem] * (many + 4),
        out_specs=(vmem,) * (many + 3),
        scratch_shapes=[
            *(
                pltpu.VMEM((lines,) + grad.shape[1:], grad.dtype)
                for _ in range(3)
                for grad in grads
            ),
            pltpu.VMEM(branch.shape, branch.dtype),
            pltpu.VMEM(feature_grad.shape, feature_grad.dtype),
            pltpu.VMEM(vectors.shape, f32),
            pltpu.VMEM((fsdp,) + vectors.shape, f32),
            pltpu.VMEM((tp, 8, vectors.shape[1]), f32),
            dma((many, lines)),
            dma((many, lines)),
            dma((many, lines)),
            dma((many, lines)),
            dma((2, tp)),
            dma((2, tp)),
            dma((fsdp,)),
            dma((fsdp,)),
            dma((tp,)),
            dma((tp,)),
        ],
        compiler_params=pltpu.CompilerParams(
            collective_id=2, has_side_effects=True, vmem_limit_bytes=56 * 1024 * 1024
        ),
        name="scatter_all",
    )(*grads, branch, feature_grad, normed, vectors)


MOST = 512
SPAN = 256


def attention_kernel(
    heads,
    f_ref,
    c_ref,
    wq_ref,
    bq_ref,
    wo_ref,
    cos_ref,
    sin_ref,
    turn_ref,
    col_ref,
    row_ref,
    o_ref,
    dx_ref,
    sum_ref,
    queries,
    keys_in,
    values_in,
    grads_in,
    mixed,
    grad_q,
    grad_k,
    grad_v,
    x_ref,
    do_ref,
):
    length = f_ref.shape[0]
    span = min(SPAN, length)
    scale = HEAD_DIM ** (-0.5)
    two = 2 * HEAD_DIM
    f32 = jnp.float32
    bf16 = jnp.bfloat16

    def turned(value, axis):
        return lax.dot_general(
            value,
            turn_ref[...],
            (((1,), (axis,)), ((), ())),
            precision=lax.Precision.HIGHEST,
            preferred_element_type=f32,
        )

    for first in range(0, length, span):
        part = slice(first, first + span)
        x_ref[part] = (
            jnp.dot(f_ref[part], wq_ref[...], preferred_element_type=f32) + bq_ref[...]
        )
        do_ref[part] = jnp.dot(c_ref[part], wo_ref[...], preferred_element_type=f32).astype(bf16)
    for n in range(heads):
        base = 3 * HEAD_DIM * n
        for first in range(0, length, span):
            part = slice(first, first + span)
            both = x_ref[part, base : base + two]
            both = both * cos_ref[part] + turned(both, 0) * sin_ref[part]
            queries[n, part] = both[:, :HEAD_DIM].astype(bf16) * bf16(scale)
            keys_in[n, part] = both[:, HEAD_DIM:].astype(bf16)
            values_in[n, part] = x_ref[part, base + two : base + two + HEAD_DIM].astype(bf16)
            grads_in[n, part] = do_ref[part, n * HEAD_DIM : (n + 1) * HEAD_DIM]
    grad_k[...] = jnp.zeros_like(grad_k)
    grad_v[...] = jnp.zeros_like(grad_v)

    def one_head(n, carry):
        for first in range(0, length, span):
            last = first + span
            low = max(0, (first - MOST) // span * span)
            part = slice(first, last)
            window = slice(low, last)
            q = queries[n, part]
            k = keys_in[n, window]
            v = values_in[n, window]
            g = grads_in[n, part]
            shape = (span, last - low)
            allowed = (col_ref[part] == row_ref[:, window]) & (
                lax.broadcasted_iota(jnp.int32, shape, 0) + first
                >= lax.broadcasted_iota(jnp.int32, shape, 1) + low
            )
            scores = jnp.where(allowed, cross_cols(q, k), -1e30)
            exps = jnp.exp(scores - jnp.max(scores, axis=-1, keepdims=True))
            probs = exps * (1.0 / jnp.sum(exps, axis=-1, keepdims=True))
            weights = probs.astype(bf16)
            out = jnp.dot(weights, v, preferred_element_type=f32).astype(bf16)
            mixed[n, part] = out
            delta = jnp.sum(g.astype(f32) * out.astype(f32), axis=-1, keepdims=True)
            grad_probs = cross_cols(g, v)
            grad_scores = (probs * (grad_probs - delta)).astype(bf16)
            grad_q[n, part] = jnp.dot(grad_scores, k, preferred_element_type=f32) * scale
            grad_k[n, window] += cross_rows(grad_scores, q)
            grad_v[n, window] += cross_rows(weights, g)
        return carry

    lax.fori_loop(0, heads, one_head, 0)

    sum_ref[...] = jnp.zeros_like(sum_ref)
    for first in range(0, length, span):
        part = slice(first, first + span)
        pieces = []
        for n in range(heads):
            both = jnp.concatenate([grad_q[n, part], grad_k[n, part]], axis=1)
            both = both * cos_ref[part] + turned(both * sin_ref[part], 1)
            pieces += [both, grad_v[n, part]]
        whole = jnp.concatenate(pieces, axis=1)
        sum_ref[...] += jnp.sum(whole, axis=0, keepdims=True)
        dx_ref[part] = whole.astype(bf16)
        o_ref[part] = jnp.concatenate([mixed[n, part] for n in range(heads)], axis=1)


def attention_branch(features, grad_rows, qkv_full, qkv_bias, out_full, segment_row):
    length = features.shape[0]
    heads = qkv_full.shape[1] // (3 * HEAD_DIM)
    cos_table, sin_table = rotary_tables(positions_of(segment_row))
    rest = ((0, 0), (0, HEAD_DIM - ROT))
    cos_full = jnp.tile(jnp.pad(cos_table, rest, constant_values=1.0), (1, 2))
    sin_full = jnp.tile(jnp.pad(sin_table, rest), (1, 2))
    half = ROT // 2
    source = jnp.arange(2 * HEAD_DIM)[:, None]
    target = jnp.arange(2 * HEAD_DIM)[None, :]
    inner = target % HEAD_DIM
    turn = jnp.where(
        (inner < half) & (source == target + half),
        -1.0,
        jnp.where((inner >= half) & (inner < ROT) & (source == target - half), 1.0, 0.0),
    ).astype(jnp.float32)
    wide = qkv_full.shape[1]
    vmem = pl.BlockSpec(memory_space=pltpu.VMEM)
    mixed_rows, packed_grad, sums = pl.pallas_call(
        functools.partial(attention_kernel, heads),
        out_shape=(
            jax.ShapeDtypeStruct((length, heads * HEAD_DIM), jnp.bfloat16),
            jax.ShapeDtypeStruct((length, wide), jnp.bfloat16),
            jax.ShapeDtypeStruct((1, wide), jnp.float32),
        ),
        in_specs=[vmem] * 10,
        out_specs=(vmem,) * 3,
        scratch_shapes=[pltpu.VMEM((heads, length, HEAD_DIM), jnp.bfloat16)] * 5
        + [pltpu.VMEM((heads, length, HEAD_DIM), jnp.float32)] * 3
        + [
            pltpu.VMEM((length, wide), jnp.float32),
            pltpu.VMEM((length, heads * HEAD_DIM), jnp.bfloat16),
        ],
        compiler_params=pltpu.CompilerParams(vmem_limit_bytes=56 * 1024 * 1024),
        name="attention",
    )(
        features,
        grad_rows,
        qkv_full,
        qkv_bias[None],
        out_full,
        cos_full,
        sin_full,
        turn,
        segment_row[:, None],
        segment_row[None, :],
    )
    return mixed_rows, packed_grad, sums[0]


def staged_body(
    layer_input,
    out_cotangent,
    segments,
    norm_gain,
    norm_bias,
    qkv_weight,
    qkv_bias,
    out_weight,
    out_bias,
    up_weight,
    up_bias,
    down_weight,
    down_bias,
):
    width_qkv = qkv_weight.shape[1]
    width_out = out_weight.shape[0]
    width_up = up_weight.shape[1]
    own_rows = layer_input.astype(jnp.float32)
    normed, inverse, shifted = layer_norm(own_rows, norm_gain, norm_bias)
    w_all, features, grad_rows = gather_all(
        jnp.concatenate([up_weight, down_weight.T, qkv_weight, out_weight.T], axis=1),
        shifted.astype(jnp.bfloat16),
        out_cotangent,
    )
    ends = (width_up, 2 * width_up, 2 * width_up + width_qkv)
    full_up, full_down, full_qkv, full_out = jnp.split(w_all, ends, axis=1)

    pre_act = jnp.dot(features, full_up, preferred_element_type=jnp.float32) + up_bias
    gelu_rows = gelu_value(pre_act).astype(jnp.bfloat16)
    grad_pre = jnp.dot(grad_rows, full_down, preferred_element_type=jnp.float32) * gelu_slope(
        pre_act
    )
    pre_grads = grad_pre.astype(jnp.bfloat16)
    up_bias_part = jnp.sum(grad_pre, axis=0)
    mixed_rows, packed_bf, qkv_bias_part = attention_branch(
        features, grad_rows, full_qkv, qkv_bias, full_out, segments[0]
    )
    branch = cross_cols(mixed_rows, full_out) + cross_cols(gelu_rows, full_down)
    feature_grad = cross_cols(packed_bf, full_qkv) + cross_cols(pre_grads, full_up)
    grads = [
        cross_rows(features, pre_grads).astype(jnp.bfloat16),
        cross_rows(grad_rows, gelu_rows).astype(jnp.bfloat16),
        cross_rows(features, packed_bf).astype(jnp.bfloat16),
        cross_rows(grad_rows, mixed_rows).astype(jnp.bfloat16),
    ]
    cot_rows = out_cotangent.astype(jnp.float32)
    model = own_rows.shape[1]
    biases = jnp.concatenate([qkv_bias_part, up_bias_part])
    bias_rows = -(-biases.shape[0] // model)
    biases = jnp.pad(biases, (0, bias_rows * model - biases.shape[0])).reshape(bias_rows, model)
    vectors = jnp.concatenate(
        [
            jnp.zeros((2, model), jnp.float32),
            jnp.sum(cot_rows, axis=0)[None],
            jnp.zeros((5, model), jnp.float32),
            biases,
            jnp.zeros((-bias_rows % 8, model), jnp.float32),
        ]
    )
    up_grad, down_grad, qkv_grad, out_grad, branch, row_grad, sums = scatter_all(
        grads,
        branch.astype(jnp.bfloat16),
        feature_grad.astype(jnp.bfloat16),
        normed,
        vectors,
    )
    layer_output = (own_rows + branch + out_bias + down_bias).astype(jnp.bfloat16)
    gain_grad, shift_grad, bias_grad = sums[0], sums[1], sums[2]
    bias_flat = sums[8 : 8 + bias_rows].reshape(-1)
    qkv_bias_grad = bias_flat[:width_qkv]
    up_bias_grad = bias_flat[width_qkv : width_qkv + width_up]
    scaled = row_grad * norm_gain
    input_grad = (
        cot_rows
        + inverse
        * (
            scaled
            - jnp.mean(scaled, axis=-1, keepdims=True)
            - normed * jnp.mean(scaled * normed, axis=-1, keepdims=True)
        )
    ).astype(jnp.bfloat16)
    return (
        layer_output,
        input_grad,
        gain_grad,
        shift_grad,
        qkv_grad,
        qkv_bias_grad,
        out_grad.T,
        bias_grad,
        up_grad,
        up_bias_grad,
        down_grad.T,
        bias_grad,
    )


DOCS = 4


def error_function(value):
    x = jnp.clip(value, -3.7439211627767994, 3.7439211627767994)
    y = x * x
    top = jnp.float32(0.00022905065861350646)
    for c in (
        0.0034082910107109506,
        0.050955695062380861,
        0.18520832239976145,
        1.128379143519084,
    ):
        top = top * y + jnp.float32(c)
    low = jnp.float32(-1.1791602954361697e-7)
    for c in (
        0.000023547966471313185,
        0.0010179625278914885,
        0.014070470171167667,
        0.11098505178285362,
        0.49746925110067538,
        1.0,
    ):
        low = low * y + jnp.float32(c)
    return x * top / low


def layer_kernel(
    fsdp,
    tp,
    heads,
    x_ref,
    c_ref,
    seg_ref,
    gain_ref,
    shift_ref,
    ob_ref,
    db_ref,
    bq_ref,
    bu_ref,
    wq_ref,
    wo_ref,
    wu_ref,
    wd_ref,
    y_out,
    dx_out,
    gq_out,
    go_out,
    gu_out,
    gd_out,
    v_out,
    w_all,
    h_all,
    c_all,
    h_turn,
    c_turn,
    normed_ref,
    inverse_ref,
    cos_ref,
    sin_a,
    sin_b,
    start_ref,
    qkv_ref,
    do_ref,
    queries,
    keys_in,
    values_in,
    grads_in,
    mixed,
    grad_q,
    grad_k,
    grad_v,
    o_ref,
    packed,
    gelu_ref,
    pre_ref,
    g_all,
    halves,
    joined,
    lands,
    part,
    mates,
    summed,
    sides_in,
    d_out,
    early,
    early_all,
    rows,
    rows_all,
    shared,
    up_send,
    down_send,
    z_recv,
    y_send,
    y_recv,
    x_send,
    x_recv,
    m_send,
    m_recv,
    a_send,
    a_recv,
    l_send,
    l_recv,
    pm_send,
    pm_recv,
    px_send,
    px_recv,
    e_send,
    e_recv,
    v_send,
    v_recv,
    u_send,
    u_recv,
):
    f32 = jnp.float32
    bf16 = jnp.bfloat16
    f, t, pair, line = place(fsdp, tp)
    lines = fsdp // 2
    sides = tp // 2
    side = lax.div(t, 2)
    par = lax.rem(t, 2)
    partner = 2 * line + 1 - pair
    mate = 2 * side + 1 - par
    block = x_ref.shape[0]
    model = x_ref.shape[1]
    shard = wu_ref.shape[0]
    hidden = wu_ref.shape[1]
    wide = wq_ref.shape[1]
    length = tp * block
    two = 2 * HEAD_DIM
    scale = HEAD_DIM ** (-0.5)
    half = ROT // 2

    barrier = pltpu.get_barrier_semaphore()
    each(
        1,
        fsdp,
        lambda step: pl.semaphore_signal(
            barrier, inc=1, device_id=(lax.rem(f + step, fsdp), t), device_id_type=MESH
        ),
    )
    each(
        1,
        tp,
        lambda step: pl.semaphore_signal(
            barrier, inc=1, device_id=(f, lax.rem(t + step, tp)), device_id_type=MESH
        ),
    )
    w_all[0, f] = jnp.concatenate([wq_ref[...], wo_ref[...]], axis=1)
    w_all[1, f] = wu_ref[...]
    w_all[2, f] = wd_ref[...]
    c_all[t] = c_ref[...]
    own = x_ref[...].astype(f32)
    normed, inverse, shifted = layer_norm(own, gain_ref[...], shift_ref[...])
    h_all[t] = shifted.astype(bf16)
    normed_ref[...] = normed
    inverse_ref[...] = inverse
    pl.semaphore_wait(barrier, fsdp + tp - 2)

    def slot(origin):
        return 2 * origin + pair

    def z_copy(i, origin, send, to):
        view = w_all.at[i, slot(origin)]
        return remote(view, view, send.at[i, origin], z_recv.at[i, origin], (2 * to + pair, t))

    def z_up(i, origin):
        return z_copy(i, origin, up_send, line + 1)

    def z_down(i, origin):
        return z_copy(i, origin, down_send, line - 1)

    def y_copy(i, origin, side_of):
        view = w_all.at[i, 2 * origin + side_of]
        return remote(view, view, y_send.at[i, origin], y_recv.at[i, origin], (partner, t))

    def send_own(i):
        @pl.when(line + 1 < lines)
        def _():
            z_up(i, line).start()

        @pl.when(line > 0)
        def _():
            z_down(i, line).start()

        y_copy(i, line, pair).start()

    def relay(r):
        i = lax.div(r, lines - 1)
        k = lax.rem(r, lines - 1) + 1
        below = line - k
        above = line + k

        @pl.when(below >= 0)
        def _():
            z_up(i, below).wait_recv()

            @pl.when(line + 1 < lines)
            def _():
                z_up(i, below).start()

            y_copy(i, below, pair).start()

        @pl.when(above < lines)
        def _():
            z_down(i, above).wait_recv()

            @pl.when(line > 0)
            def _():
                z_down(i, above).start()

            y_copy(i, above, pair).start()

    relays = 3 * (lines - 1)

    tokens = (h_all, c_all)

    def x_copy(which, step, place_of):
        view = tokens[which].at[place_of]
        other = lax.rem(side + step, sides)
        return remote(
            view, view, x_send.at[which, step], x_recv.at[which, step], (f, 2 * other + par)
        )

    def m_copy(which, origin, parity):
        view = tokens[which].at[2 * origin + parity]
        return remote(
            view, view, m_send.at[which, origin], m_recv.at[which, origin], (f, mate)
        )

    def arrive(which):
        def one(step):
            origin = lax.rem(side + sides - step, sides)
            x_copy(which, step, 2 * origin + par).wait_recv()
            m_copy(which, origin, par).start()

        each(1, sides, one)

    def settle(which):
        each(0, sides, lambda origin: m_copy(which, origin, 1 - par).wait_recv())

    each(1, sides, lambda step: x_copy(0, step, t).start())
    send_own(0)
    m_copy(0, side, par).start()
    each(1, sides, lambda step: x_copy(1, step, t).start())
    m_copy(1, side, par).start()
    send_own(1)

    seg = seg_ref[...]
    down_rows = lax.broadcasted_iota(jnp.int32, (length, 1), 0)
    along_row = lax.broadcasted_iota(jnp.int32, (1, length), 1)
    start_col = jnp.zeros((length, 1), jnp.int32)
    start_row = jnp.zeros((1, length), jnp.int32)
    for d in range(1, DOCS):
        count = jnp.sum((seg < d).astype(jnp.int32), axis=1, keepdims=True)
        start_col = jnp.where(down_rows >= count, count, start_col)
        start_row = jnp.where(along_row >= count, count, start_row)
    start_ref[...] = start_col
    spot = (along_row - start_row).astype(f32)
    order = lax.broadcasted_iota(jnp.int32, (half, 1), 0).astype(f32)
    rates = jnp.exp(order * (-2.0 / ROT * 9.210340371976184))
    angles = spot * rates
    lane = lax.broadcasted_iota(jnp.int32, (half, two), 1) % HEAD_DIM
    pick = lax.broadcasted_iota(jnp.int32, (half, two), 0)
    first_half = (lane == pick).astype(f32)
    last_half = (lane == pick + half).astype(f32)

    def spread_out(table, matrix):
        return lax.dot_general(
            table,
            matrix,
            (((0,), (0,)), ((), ())),
            precision=lax.Precision.HIGHEST,
            preferred_element_type=f32,
        )

    cosine = jnp.cos(angles)
    sine = jnp.sin(angles)
    beyond = lax.broadcasted_iota(jnp.int32, (1, two), 1) % HEAD_DIM >= ROT
    cos_ref[...] = jnp.where(beyond, 1.0, spread_out(cosine, first_half + last_half))
    sin_a[...] = spread_out(sine, last_half)
    sin_b[...] = -spread_out(sine, first_half)

    each(0, lines - 1, relay)
    send_own(2)
    arrive(0)
    ahead_of = (lines - 1) + min(2, lines - 1)
    relay(lines - 1)
    settle(0)
    for s in range(tp):
        h_turn[:, s * block : (s + 1) * block] = h_all[s].T
    each(lines, ahead_of, relay)
    each(0, lines, lambda origin: y_copy(0, origin, 1 - pair).wait_recv())

    def project_q(s, carry):
        weight = w_all[0].reshape(model, model)
        part_of = pl.ds(s * block, block)
        qkv_ref[part_of] = (
            jnp.dot(h_all[s], weight[:, :wide], preferred_element_type=f32) + bq_ref[...]
        )
        return carry

    lax.fori_loop(0, tp, project_q, 0)
    arrive(1)

    def rotated(value, spots, sign):
        return (
            value * cos_ref[spots]
            + sign
            * (
                pltpu.roll(value, half, 1) * sin_a[spots]
                + pltpu.roll(value, two - half, 1) * sin_b[spots]
            )
        )

    for n in range(heads):
        base = 3 * HEAD_DIM * n

        def prepare(s, carry, n=n, base=base):
            spots = pl.ds(s * block, block)
            both = rotated(qkv_ref[spots, base : base + two], spots, 1.0)
            queries[n, spots] = both[:, :HEAD_DIM].astype(bf16) * bf16(scale)
            keys_in[n, spots] = both[:, HEAD_DIM:].astype(bf16)
            values_in[n, spots] = qkv_ref[spots, base + two : base + two + HEAD_DIM].astype(bf16)
            return carry

        lax.fori_loop(0, tp, prepare, 0)
    settle(1)
    for s in range(tp):
        c_turn[:, s * block : (s + 1) * block] = c_all[s].T

    def project_o(s, carry):
        weight = w_all[0].reshape(model, model)
        spots = pl.ds(s * block, block)
        value = jnp.dot(c_all[s], weight[:, wide:], preferred_element_type=f32).astype(bf16)
        for n in range(heads):
            grads_in[n, spots] = value[:, n * HEAD_DIM : (n + 1) * HEAD_DIM]
        return carry

    lax.fori_loop(0, tp, project_o, 0)
    grad_k[...] = jnp.zeros_like(grad_k)
    grad_v[...] = jnp.zeros_like(grad_v)
    span = min(SPAN, length)
    parts = length // span
    steps = heads * parts
    busy = max(1, steps * 3 // 4)
    left = relays - ahead_of

    def due(j):
        return ahead_of + jnp.minimum(left, lax.div(j * left, busy))

    def one_head(n, carry):
        for m in range(parts):
            first = m * span
            last = first + span
            low = max(0, (first - MOST) // span * span)
            spots = slice(first, last)
            window = slice(low, last)
            q = queries[n, spots]
            k = keys_in[n, window]
            v = values_in[n, window]
            g = grads_in[n, spots]
            shape = (span, last - low)
            key_at = lax.broadcasted_iota(jnp.int32, shape, 1) + low
            allowed = (key_at >= start_ref[spots]) & (
                lax.broadcasted_iota(jnp.int32, shape, 0) + first >= key_at
            )
            scores = jnp.where(allowed, cross_cols(q, k), -1e30)
            exps = jnp.exp(scores - jnp.max(scores, axis=-1, keepdims=True))
            probs = exps * (1.0 / jnp.sum(exps, axis=-1, keepdims=True))
            weights = probs.astype(bf16)
            out = jnp.dot(weights, v, preferred_element_type=f32).astype(bf16)
            mixed[n, spots] = out
            delta = jnp.sum(g.astype(f32) * out.astype(f32), axis=-1, keepdims=True)
            grad_probs = cross_cols(g, v)
            grad_scores = (probs * (grad_probs - delta)).astype(bf16)
            grad_q[n, spots] = jnp.dot(grad_scores, k, preferred_element_type=f32) * scale
            grad_k[n, window] += cross_rows(grad_scores, q)
            grad_v[n, window] += cross_rows(weights, g)
            j = n * parts + m
            each(due(j), due(j + 1), relay)
        return carry

    lax.fori_loop(0, heads, one_head, 0)

    early[...] = jnp.zeros_like(early)

    def finish(s, carry):
        spots = pl.ds(s * block, block)
        pieces = []
        for n in range(heads):
            both = jnp.concatenate([grad_q[n, spots], grad_k[n, spots]], axis=1)
            pieces += [rotated(both, spots, -1.0), grad_v[n, spots]]
        whole = jnp.concatenate(pieces, axis=1)
        early[0:1, :wide] += jnp.sum(whole, axis=0, keepdims=True)
        packed[spots] = whole.astype(bf16)
        o_ref[spots] = jnp.concatenate([mixed[n, spots] for n in range(heads)], axis=1)
        return carry

    lax.fori_loop(0, tp, finish, 0)

    def ahead(step):
        return lax.rem(line + step, lines)

    def across(i, step):
        return remote(
            g_all.at[i, 2 * ahead(step) + 1 - pair],
            halves.at[i, step],
            a_send.at[i, step],
            a_recv.at[i, step],
            (partner, t),
        )

    def along(i, step):
        return remote(
            joined.at[i, step],
            lands.at[i, step],
            l_send.at[i, step],
            l_recv.at[i, step],
            (2 * ahead(step) + pair, t),
        )

    def start_across(i):
        each(1, lines, lambda step: across(i, step).start())
        across(i, 0).start()

    def join(i, step):
        across(i, step).wait_recv()
        joined[i, step] = (
            g_all[i, 2 * ahead(step) + pair].astype(f32) + halves[i, step].astype(f32)
        ).astype(bf16)
        along(i, step).start()

    tile = model // 2
    many = tile // shard

    def store_grad(i, j, value):
        g_all[i, pl.ds(j * many, many)] = value.astype(bf16).reshape(many, shard, value.shape[1])

    def grad_attention(j, carry):
        spots = pl.ds(j * tile, tile)
        store_grad(
            0,
            j,
            jnp.concatenate(
                [
                    jnp.dot(h_turn[spots], packed[...], preferred_element_type=f32),
                    jnp.dot(c_turn[spots], o_ref[...], preferred_element_type=f32),
                ],
                axis=1,
            ),
        )
        return carry

    def grad_up(j, carry):
        store_grad(
            1,
            j,
            jnp.dot(h_turn[pl.ds(j * tile, tile)], pre_ref[...], preferred_element_type=f32),
        )
        return carry

    def grad_down(j, carry):
        store_grad(
            2,
            j,
            jnp.dot(c_turn[pl.ds(j * tile, tile)], gelu_ref[...], preferred_element_type=f32),
        )
        return carry

    lax.fori_loop(0, 2, grad_attention, 0)
    start_across(0)

    each(due(steps), relays, relay)
    each(0, lines, lambda origin: y_copy(1, origin, 1 - pair).wait_recv())
    each(0, lines, lambda origin: y_copy(2, origin, 1 - pair).wait_recv())

    def hidden_rows(s, carry):
        spots = pl.ds(s * block, block)
        up = w_all[1].reshape(model, hidden)
        down = w_all[2].reshape(model, hidden)
        a = jnp.dot(h_all[s], up, preferred_element_type=f32) + bu_ref[...]
        bell = 0.5 * (1.0 + error_function(a * 0.7071067811865476))
        gelu_ref[spots] = (a * bell).astype(bf16)
        slope = bell + a * jnp.exp(-0.5 * a * a) * 0.3989422804014327
        grad = jnp.dot(c_all[s], down, preferred_element_type=f32) * slope
        early[1:2, :hidden] += jnp.sum(grad, axis=0, keepdims=True)
        pre_ref[spots] = grad.astype(bf16)
        return carry

    lax.fori_loop(0, tp, hidden_rows, 0)

    def e_copy(step, place_of):
        return remote(
            early,
            early_all.at[place_of],
            e_send.at[step],
            e_recv.at[step],
            (lax.rem(f + step, fsdp), t),
        )

    early[2:3] = jnp.sum(c_all[t].astype(f32), axis=0, keepdims=True)
    join(0, 1)
    lax.fori_loop(0, 2, grad_up, 0)
    start_across(1)
    each(1, fsdp, lambda step: e_copy(step, f).start())
    join(0, 2)

    def pm_copy(which, origin):
        return remote(
            part.at[which, 2 * origin + 1 - par],
            mates.at[which, origin],
            pm_send.at[which, origin],
            pm_recv.at[which, origin],
            (f, mate),
        )

    def px_copy(which, step):
        other = lax.rem(side + step, sides)
        return remote(
            summed.at[which, step],
            sides_in.at[which, step],
            px_send.at[which, step],
            px_recv.at[which, step],
            (f, 2 * other + par),
        )

    def feature_rows(s, carry):
        spots = pl.ds(s * block, block)
        weight = w_all[0].reshape(model, model)
        part[0, s] = (
            cross_cols(packed[spots], weight[:, :wide])
            + cross_cols(pre_ref[spots], w_all[1].reshape(model, hidden))
        ).astype(bf16)
        return carry

    def branch_rows(s, carry):
        spots = pl.ds(s * block, block)
        weight = w_all[0].reshape(model, model)
        part[1, s] = (
            cross_cols(o_ref[spots], weight[:, wide:])
            + cross_cols(gelu_ref[spots], w_all[2].reshape(model, hidden))
        ).astype(bf16)
        return carry

    def pass_on(which):
        def one(step):
            other = lax.rem(side + step, sides)
            pm_copy(which, other).wait_recv()
            summed[which, step] = (
                part[which, 2 * other + par].astype(f32) + mates[which, other].astype(f32)
            ).astype(bf16)
            px_copy(which, step).start()

        each(1, sides, one)

    def gathered(which):
        pm_copy(which, side).wait_recv()
        d_out[...] = part[which, t].astype(f32) + mates[which, side].astype(f32)

        def one(step):
            px_copy(which, step).wait_recv()
            d_out[...] += sides_in[which, step].astype(f32)

        each(1, sides, one)

    lax.fori_loop(0, tp, feature_rows, 0)
    each(0, sides, lambda origin: pm_copy(0, origin).start())
    each(3, lines, lambda step: join(0, step))
    lax.fori_loop(0, 2, grad_down, 0)
    start_across(2)
    pass_on(0)
    lax.fori_loop(0, tp, branch_rows, 0)
    each(0, sides, lambda origin: pm_copy(1, origin).start())
    join(1, 1)
    pass_on(1)
    each(2, lines, lambda step: join(1, step))

    gathered(0)
    rows[...] = jnp.zeros_like(rows)
    rows[0:1] = jnp.sum(d_out[...] * normed_ref[...], axis=0, keepdims=True)
    rows[1:2] = jnp.sum(d_out[...], axis=0, keepdims=True)
    each(1, fsdp, lambda step: e_copy(step, lax.rem(f + fsdp - step, fsdp)).wait_recv())
    early_all[f] = early[...]
    total = lax.fori_loop(1, fsdp, lambda step, value: value + early_all[step], early_all[0])
    v_out[8:16] = total
    rows[2:3] = early[2:3]

    def v_copy(step, place_of):
        return remote(
            rows,
            rows_all.at[place_of],
            v_send.at[step],
            v_recv.at[step],
            (lax.rem(f + step, fsdp), t),
        )

    each(1, fsdp, lambda step: v_copy(step, f).start())
    rows_all[f] = rows[...]
    normed = normed_ref[...]
    scaled = d_out[...] * gain_ref[...]
    dx_out[...] = (
        c_ref[...].astype(f32)
        + inverse_ref[...]
        * (
            scaled
            - jnp.mean(scaled, axis=-1, keepdims=True)
            - normed * jnp.mean(scaled * normed, axis=-1, keepdims=True)
        )
    ).astype(bf16)
    join(2, 1)
    each(1, fsdp, lambda step: v_copy(step, lax.rem(f + fsdp - step, fsdp)).wait_recv())
    shared[t] = lax.fori_loop(1, fsdp, lambda step, value: value + rows_all[step], rows_all[0])

    def u_copy(step, place_of):
        view = shared.at[place_of]
        return remote(
            shared.at[t],
            view,
            u_send.at[step],
            u_recv.at[step],
            (f, lax.rem(t + step, tp)),
        )

    each(1, tp, lambda step: u_copy(step, t).start())
    each(2, lines, lambda step: join(2, step))
    gathered(1)
    y_out[...] = (x_ref[...].astype(f32) + d_out[...] + ob_ref[...] + db_ref[...]).astype(bf16)
    each(1, tp, lambda step: u_copy(step, lax.rem(t + tp - step, tp)).wait_recv())
    whole = shared[0]
    for step in range(1, tp):
        whole = whole + shared[step]
    v_out[0:8] = whole

    def collected(i):
        across(i, 0).wait_recv()
        value = g_all[i, f].astype(f32) + halves[i, 0].astype(f32)

        def one(step, value):
            along(i, step).wait_recv()
            return value + lands[i, step].astype(f32)

        return lax.fori_loop(1, lines, one, value)

    value = collected(0)
    gq_out[...] = value[:, :wide]
    go_out[...] = value[:, wide:]
    gu_out[...] = collected(1)
    gd_out[...] = collected(2)

    for i in range(3):

        @pl.when(line + 1 < lines)
        def _():
            each(0, line + 1, lambda origin: z_up(i, origin).wait_send())

        @pl.when(line > 0)
        def _():
            each(line, lines, lambda origin: z_down(i, origin).wait_send())

        each(0, lines, lambda origin: y_copy(i, origin, pair).wait_send())
        each(0, lines, lambda step: across(i, step).wait_send())
        each(1, lines, lambda step: along(i, step).wait_send())
    for which in range(2):
        each(1, sides, lambda step: x_copy(which, step, t).wait_send())
        each(0, sides, lambda origin: m_copy(which, origin, par).wait_send())
        each(0, sides, lambda origin: pm_copy(which, origin).wait_send())
        each(1, sides, lambda step: px_copy(which, step).wait_send())
    each(1, fsdp, lambda step: e_copy(step, f).wait_send())
    each(1, fsdp, lambda step: v_copy(step, f).wait_send())
    each(1, tp, lambda step: u_copy(step, t).wait_send())


def layer_call(x, c, seg, gain, shift, ob, db, bq, bu, wq, wo, wu, wd):
    fsdp = lax.axis_size("fsdp")
    tp = lax.axis_size("tp")
    lines = fsdp // 2
    sides = tp // 2
    block, model = x.shape
    shard, hidden = wu.shape
    wide = wq.shape[1]
    heads = wide // (3 * HEAD_DIM)
    length = tp * block
    two = 2 * HEAD_DIM
    f32 = jnp.float32
    bf16 = jnp.bfloat16
    vmem = pl.BlockSpec(memory_space=pltpu.VMEM)
    dma = pltpu.SemaphoreType.DMA
    buf = pltpu.VMEM
    return pl.pallas_call(
        functools.partial(layer_kernel, fsdp, tp, heads),
        out_shape=(
            jax.ShapeDtypeStruct((block, model), bf16),
            jax.ShapeDtypeStruct((block, model), bf16),
            jax.ShapeDtypeStruct((shard, wide), f32),
            jax.ShapeDtypeStruct((shard, model - wide), f32),
            jax.ShapeDtypeStruct((shard, hidden), f32),
            jax.ShapeDtypeStruct((shard, hidden), f32),
            jax.ShapeDtypeStruct((16, model), f32),
        ),
        in_specs=[vmem] * 13,
        out_specs=(vmem,) * 7,
        scratch_shapes=[
            buf((3, fsdp, shard, model), bf16),
            buf((tp, block, model), bf16),
            buf((tp, block, model), bf16),
            buf((model, length), bf16),
            buf((model, length), bf16),
            buf((block, model), f32),
            buf((block, 1), f32),
            buf((length, two), f32),
            buf((length, two), f32),
            buf((length, two), f32),
            buf((length, 1), jnp.int32),
            buf((length, wide), f32),
            buf((8, 128), f32),
        ]
        + [buf((heads, length, HEAD_DIM), bf16)] * 5
        + [buf((heads, length, HEAD_DIM), f32)] * 3
        + [
            buf((length, heads * HEAD_DIM), bf16),
            buf((length, wide), bf16),
            buf((length, hidden), bf16),
            buf((length, hidden), bf16),
            buf((3, fsdp, shard, model), bf16),
            buf((3, lines, shard, model), bf16),
            buf((3, lines, shard, model), bf16),
            buf((3, lines, shard, model), bf16),
            buf((2, tp, block, model), bf16),
            buf((2, sides, block, model), bf16),
            buf((2, sides, block, model), bf16),
            buf((2, sides, block, model), bf16),
            buf((block, model), f32),
            buf((8, model), f32),
            buf((fsdp, 8, model), f32),
            buf((8, model), f32),
            buf((fsdp, 8, model), f32),
            buf((tp, 8, model), f32),
        ]
        + [dma((3, lines))] * 5
        + [dma((2, sides))] * 4
        + [dma((3, lines))] * 4
        + [dma((2, sides))] * 4
        + [dma((fsdp,))] * 4
        + [dma((tp,))] * 2,
        compiler_params=pltpu.CompilerParams(
            collective_id=3, has_side_effects=True, vmem_limit_bytes=62 * 1024 * 1024
        ),
        name="layer",
    )(x, c, seg, gain, shift, ob, db, bq, bu, wq, wo, wu, wd)


def fused_body(
    layer_input,
    out_cotangent,
    segments,
    norm_gain,
    norm_bias,
    qkv_weight,
    qkv_bias,
    out_weight,
    out_bias,
    up_weight,
    up_bias,
    down_weight,
    down_bias,
):
    y, dx, qkv_grad, out_grad, up_grad, down_grad, sums = layer_call(
        layer_input,
        out_cotangent,
        segments,
        norm_gain[None],
        norm_bias[None],
        out_bias[None],
        down_bias[None],
        qkv_bias[None],
        up_bias[None],
        qkv_weight,
        out_weight.T,
        up_weight,
        down_weight.T,
    )
    return (
        y,
        dx,
        sums[0],
        sums[1],
        qkv_grad,
        sums[8, : qkv_bias.shape[0]],
        out_grad.T,
        sums[2],
        up_grad,
        sums[9, : up_bias.shape[0]],
        down_grad.T,
        sums[2],
    )


def body(*args):
    rows = args[5].shape[0]
    model, hidden = args[9].shape[0] * lax.axis_size("fsdp"), args[9].shape[1]
    fits = (
        rows % 16 == 0
        and (model // 2) % rows == 0
        and args[5].shape[1] + args[7].shape[0] == model == hidden
        and args[2].shape == (1, lax.axis_size("tp") * args[0].shape[0])
        and args[0].shape[0] == SPAN
    )
    return fused_body(*args) if fits else staged_body(*args)


def solution(mesh):
    in_specs = (
        P(("fsdp", "tp"), None),
        P(("fsdp", "tp"), None),
        P("fsdp", None),
        P(),
        P(),
        P("fsdp", "tp"),
        P("tp"),
        P("tp", "fsdp"),
        P(),
        P("fsdp", "tp"),
        P("tp"),
        P("tp", "fsdp"),
        P(),
    )
    out_specs = (
        P(("fsdp", "tp"), None),
        P(("fsdp", "tp"), None),
        P(),
        P(),
        P("fsdp", "tp"),
        P("tp"),
        P("tp", "fsdp"),
        P(),
        P("fsdp", "tp"),
        P("tp"),
        P("tp", "fsdp"),
        P(),
    )
    return jax.shard_map(body, mesh=mesh, in_specs=in_specs, out_specs=out_specs, check_vma=False)
```

```python
import functools

import jax
import jax.numpy as jnp
from jax import lax
from jax.experimental import pallas as pl
from jax.experimental.pallas import tpu as pltpu
from jax.sharding import PartitionSpec as P

HEAD_DIM = 64
ROT = 16


EPSILON = 1e-05
ROTARY_BASE = 10000.0


def layer_norm(values, gain, shift):
    center = values - jnp.mean(values, axis=-1, keepdims=True)
    spread = jnp.mean(center * center, axis=-1, keepdims=True)
    inverse = lax.rsqrt(spread + EPSILON)
    normed = center * inverse
    return (normed, inverse, normed * gain + shift)


def gelu_value(pre_act):
    return 0.5 * pre_act * (1.0 + lax.erf(pre_act * 0.7071067811865476))


def gelu_slope(pre_act):
    return (
        0.5 * (1.0 + lax.erf(pre_act * 0.7071067811865476))
        + pre_act * jnp.exp(-0.5 * pre_act * pre_act) * 0.3989422804014327
    )


def positions_of(segment_row):
    length = segment_row.shape[0]
    counter = jnp.arange(length, dtype=jnp.int32)
    is_start = jnp.concatenate(
        [jnp.ones((1,), dtype=jnp.bool_), segment_row[1:] != segment_row[:-1]]
    )
    starts = lax.cummax(jnp.where(is_start, counter, jnp.zeros_like(counter)), axis=0)
    return counter - starts


def rotary_tables(positions):
    halves = ROT // 2
    inverse_freq = ROTARY_BASE ** (-(jnp.arange(halves, dtype=jnp.float32) * 2.0) / ROT)
    angles = positions.astype(jnp.float32)[:, None] * inverse_freq[None, :]
    cos_table = jnp.cos(angles)
    sin_table = jnp.sin(angles)
    return (
        jnp.concatenate([cos_table, cos_table], axis=-1),
        jnp.concatenate([sin_table, sin_table], axis=-1),
    )


def cross_rows(left, right):
    return lax.dot_general(
        left, right, (((0,), (0,)), ((), ())), preferred_element_type=jnp.float32
    )


def cross_cols(left, right):
    return lax.dot_general(
        left, right, (((1,), (1,)), ((), ())), preferred_element_type=jnp.float32
    )


MESH = pl.DeviceIdType.MESH


def place(fsdp, tp):
    f = lax.axis_index("fsdp")
    t = lax.axis_index("tp")
    pair = lax.rem(f, 2)
    line = lax.div(f, 2)
    return f, t, pair, line


def remote(source, target, send, recv, device):
    return pltpu.make_async_remote_copy(
        src_ref=source,
        dst_ref=target,
        send_sem=send,
        recv_sem=recv,
        device_id=device,
        device_id_type=MESH,
    )


def each(first, last, action):
    def step_of(step, carry):
        action(step)
        return carry

    lax.fori_loop(first, last, step_of, 0)


def greet(fsdp, tp):
    f, t, _, _ = place(fsdp, tp)
    barrier = pltpu.get_barrier_semaphore()
    each(
        1,
        fsdp,
        lambda step: pl.semaphore_signal(
            barrier, inc=1, device_id=(lax.rem(f + step, fsdp), t), device_id_type=MESH
        ),
    )
    each(
        1,
        tp,
        lambda step: pl.semaphore_signal(
            barrier, inc=1, device_id=(f, lax.rem(t + step, tp)), device_id_type=MESH
        ),
    )
    pl.semaphore_wait(barrier, fsdp + tp - 2)


def gather_kernel(
    fsdp, tp, w_ref, h_ref, c_ref, w_out, h_out, c_out, w_send, w_recv, p_send, p_recv, r_send, r_recv
):
    f, t, pair, line = place(fsdp, tp)
    lines = fsdp // 2
    greet(fsdp, tp)
    partner = 2 * line + 1 - pair

    def along(step, slot):
        other = lax.rem(line + step, lines)
        return remote(
            w_ref, w_out.at[slot], w_send.at[step], w_recv.at[step], (2 * other + pair, t)
        )

    def across(step, source, slot):
        return remote(source, w_out.at[slot], p_send.at[step], p_recv.at[step], (partner, t))

    def beside(step, which, source, target, slot):
        return remote(
            source,
            target.at[slot],
            r_send.at[which, step],
            r_recv.at[which, step],
            (f, lax.rem(t + step, tp)),
        )

    def came(step, side):
        return 2 * lax.rem(line + lines - step, lines) + side

    across(0, w_ref, f).start()
    each(1, lines, lambda step: along(step, f).start())
    each(1, tp, lambda step: beside(step, 0, h_ref, h_out, t).start())
    each(1, tp, lambda step: beside(step, 1, c_ref, c_out, t).start())
    w_out[f] = w_ref[...]
    h_out[t] = h_ref[...]
    c_out[t] = c_ref[...]

    def forward(step):
        slot = came(step, pair)
        along(step, slot).wait_recv()
        across(step, w_out.at[slot], slot).start()

    each(1, lines, forward)

    def settle(step):
        slot = lax.rem(t + tp - step, tp)
        beside(step, 0, h_ref, h_out, slot).wait()
        beside(step, 1, c_ref, c_out, slot).wait()

    each(1, tp, settle)
    each(1, lines, lambda step: along(step, f).wait_send())

    def finish(step):
        across(step, w_ref, came(step, 1 - pair)).wait()

    each(0, lines, finish)


def gather_all(weights, features, cotangent):
    fsdp = lax.axis_size("fsdp")
    tp = lax.axis_size("tp")
    vmem = pl.BlockSpec(memory_space=pltpu.VMEM)
    shapes = (
        jax.ShapeDtypeStruct((fsdp,) + weights.shape, weights.dtype),
        jax.ShapeDtypeStruct((tp,) + features.shape, features.dtype),
        jax.ShapeDtypeStruct((tp,) + cotangent.shape, cotangent.dtype),
    )
    dma = pltpu.SemaphoreType.DMA
    w_all, h_all, c_all = pl.pallas_call(
        functools.partial(gather_kernel, fsdp, tp),
        out_shape=shapes,
        in_specs=[vmem] * 3,
        out_specs=(vmem,) * 3,
        scratch_shapes=[
            dma((fsdp // 2,)),
            dma((fsdp // 2,)),
            dma((fsdp // 2,)),
            dma((fsdp // 2,)),
            dma((2, tp)),
            dma((2, tp)),
        ],
        compiler_params=pltpu.CompilerParams(
            collective_id=1, has_side_effects=True, vmem_limit_bytes=48 * 1024 * 1024
        ),
        name="gather_all",
    )(weights, features, cotangent)
    return (
        w_all.reshape(fsdp * weights.shape[0], weights.shape[1]),
        h_all.reshape(tp * features.shape[0], features.shape[1]),
        c_all.reshape(tp * cotangent.shape[0], cotangent.shape[1]),
    )


def scatter_kernel(
    fsdp,
    tp,
    many,
    *refs,
):
    g_refs, refs = refs[:many], refs[many:]
    b_ref, d_ref, n_ref, v_ref = refs[:4]
    g_outs, refs = refs[4 : 4 + many], refs[4 + many :]
    b_out, d_out, v_out = refs[:3]
    halves, joined, lands = (refs[3 + many * i : 3 + many * (i + 1)] for i in range(3))
    (
        b_land,
        d_land,
        rows,
        first,
        second,
        p_send,
        p_recv,
        w_send,
        w_recv,
        r_send,
        r_recv,
        v_send,
        v_recv,
        u_send,
        u_recv,
    ) = refs[3 + 3 * many :]
    f, t, pair, line = place(fsdp, tp)
    lines = fsdp // 2
    greet(fsdp, tp)
    partner = 2 * line + 1 - pair

    def ahead(step):
        return lax.rem(line + step, lines)

    def across(i, step):
        return remote(
            g_refs[i].at[2 * ahead(step) + 1 - pair],
            halves[i].at[step],
            p_send.at[i, step],
            p_recv.at[i, step],
            (partner, t),
        )

    def along(i, step):
        return remote(
            joined[i].at[step],
            lands[i].at[step],
            w_send.at[i, step],
            w_recv.at[i, step],
            (2 * ahead(step) + pair, t),
        )

    def beside(step, which, source, target):
        return remote(
            source.at[lax.rem(t + step, tp)],
            target.at[step],
            r_send.at[which, step],
            r_recv.at[which, step],
            (f, lax.rem(t + step, tp)),
        )

    def start_beside(step):
        beside(step, 1, d_ref, d_land).start()
        beside(step, 0, b_ref, b_land).start()

    def start_across(step):
        for i in range(many):
            across(i, step).start()

    each(1, lines, start_across)
    start_across(0)
    each(1, tp, start_beside)

    def join(step):
        for i in range(many):
            across(i, step).wait_recv()
            joined[i][step] = (
                g_refs[i][2 * ahead(step) + pair].astype(jnp.float32)
                + halves[i][step].astype(jnp.float32)
            ).astype(joined[i].dtype)
            along(i, step).start()

    each(1, lines, join)
    for i in range(many):
        across(i, 0).wait_recv()
        g_outs[i][...] = g_refs[i][f].astype(jnp.float32) + halves[i][0].astype(jnp.float32)

    d_out[...] = d_ref[t].astype(jnp.float32)
    b_out[...] = b_ref[t].astype(jnp.float32)

    def gather_d(step):
        beside(step, 1, d_ref, d_land).wait()
        d_out[...] += d_land[step].astype(jnp.float32)

    def gather_b(step):
        beside(step, 0, b_ref, b_land).wait()
        b_out[...] += b_land[step].astype(jnp.float32)

    each(1, tp, gather_d)
    rows[...] = v_ref[...]
    rows[0:1] = jnp.sum(d_out[...] * n_ref[...], axis=0, keepdims=True)
    rows[1:2] = jnp.sum(d_out[...], axis=0, keepdims=True)

    def spread(step, slot):
        return remote(
            rows,
            first.at[slot],
            v_send.at[step],
            v_recv.at[step],
            (lax.rem(f + step, fsdp), t),
        )

    each(1, fsdp, lambda step: spread(step, f).start())
    first[f] = rows[...]
    each(1, tp, gather_b)

    def collect(step):
        for i in range(many):
            along(i, step).wait_recv()
            g_outs[i][...] += lands[i][step].astype(jnp.float32)

    each(1, lines, collect)
    each(1, fsdp, lambda step: spread(step, lax.rem(f + fsdp - step, fsdp)).wait())
    total = lax.fori_loop(1, fsdp, lambda step, value: value + first[step], first[0])
    second[t] = total[:8]
    v_out[...] = total

    def share(step, slot):
        return remote(
            second.at[t],
            second.at[slot],
            u_send.at[step],
            u_recv.at[step],
            (f, lax.rem(t + step, tp)),
        )

    each(1, tp, lambda step: share(step, t).start())

    def sent_along(step):
        for i in range(many):
            along(i, step).wait_send()

    def sent_across(step):
        for i in range(many):
            across(i, step).wait_send()

    each(1, lines, sent_along)
    each(0, lines, sent_across)
    each(1, tp, lambda step: share(step, lax.rem(t + tp - step, tp)).wait())
    whole = second[0]
    for step in range(1, tp):
        whole = whole + second[step]
    v_out[:8] = whole


def scatter_all(grads, branch, feature_grad, normed, vectors):
    fsdp = lax.axis_size("fsdp")
    tp = lax.axis_size("tp")
    lines = fsdp // 2
    grads = [grad.reshape(fsdp, -1, grad.shape[1]) for grad in grads]
    many = len(grads)
    branch = branch.reshape(tp, -1, branch.shape[1])
    feature_grad = feature_grad.reshape(tp, -1, feature_grad.shape[1])
    vmem = pl.BlockSpec(memory_space=pltpu.VMEM)
    dma = pltpu.SemaphoreType.DMA
    f32 = jnp.float32
    return pl.pallas_call(
        functools.partial(scatter_kernel, fsdp, tp, many),
        out_shape=(
            *(jax.ShapeDtypeStruct(grad.shape[1:], f32) for grad in grads),
            jax.ShapeDtypeStruct(branch.shape[1:], f32),
            jax.ShapeDtypeStruct(feature_grad.shape[1:], f32),
            jax.ShapeDtypeStruct(vectors.shape, f32),
        ),
        in_specs=[vmem] * (many + 4),
        out_specs=(vmem,) * (many + 3),
        scratch_shapes=[
            *(
                pltpu.VMEM((lines,) + grad.shape[1:], grad.dtype)
                for _ in range(3)
                for grad in grads
            ),
            pltpu.VMEM(branch.shape, branch.dtype),
            pltpu.VMEM(feature_grad.shape, feature_grad.dtype),
            pltpu.VMEM(vectors.shape, f32),
            pltpu.VMEM((fsdp,) + vectors.shape, f32),
            pltpu.VMEM((tp, 8, vectors.shape[1]), f32),
            dma((many, lines)),
            dma((many, lines)),
            dma((many, lines)),
            dma((many, lines)),
            dma((2, tp)),
            dma((2, tp)),
            dma((fsdp,)),
            dma((fsdp,)),
            dma((tp,)),
            dma((tp,)),
        ],
        compiler_params=pltpu.CompilerParams(
            collective_id=2, has_side_effects=True, vmem_limit_bytes=56 * 1024 * 1024
        ),
        name="scatter_all",
    )(*grads, branch, feature_grad, normed, vectors)


MOST = 512
SPAN = 256


def attention_kernel(
    heads,
    f_ref,
    c_ref,
    wq_ref,
    bq_ref,
    wo_ref,
    cos_ref,
    sin_ref,
    turn_ref,
    col_ref,
    row_ref,
    o_ref,
    dx_ref,
    sum_ref,
    queries,
    keys_in,
    values_in,
    grads_in,
    mixed,
    grad_q,
    grad_k,
    grad_v,
    x_ref,
    do_ref,
):
    length = f_ref.shape[0]
    span = min(SPAN, length)
    scale = HEAD_DIM ** (-0.5)
    two = 2 * HEAD_DIM
    f32 = jnp.float32
    bf16 = jnp.bfloat16

    def turned(value, axis):
        return lax.dot_general(
            value,
            turn_ref[...],
            (((1,), (axis,)), ((), ())),
            precision=lax.Precision.HIGHEST,
            preferred_element_type=f32,
        )

    for first in range(0, length, span):
        part = slice(first, first + span)
        x_ref[part] = (
            jnp.dot(f_ref[part], wq_ref[...], preferred_element_type=f32) + bq_ref[...]
        )
        do_ref[part] = jnp.dot(c_ref[part], wo_ref[...], preferred_element_type=f32).astype(bf16)
    for n in range(heads):
        base = 3 * HEAD_DIM * n
        for first in range(0, length, span):
            part = slice(first, first + span)
            both = x_ref[part, base : base + two]
            both = both * cos_ref[part] + turned(both, 0) * sin_ref[part]
            queries[n, part] = both[:, :HEAD_DIM].astype(bf16) * bf16(scale)
            keys_in[n, part] = both[:, HEAD_DIM:].astype(bf16)
            values_in[n, part] = x_ref[part, base + two : base + two + HEAD_DIM].astype(bf16)
            grads_in[n, part] = do_ref[part, n * HEAD_DIM : (n + 1) * HEAD_DIM]
    grad_k[...] = jnp.zeros_like(grad_k)
    grad_v[...] = jnp.zeros_like(grad_v)

    def one_head(n, carry):
        for first in range(0, length, span):
            last = first + span
            low = max(0, (first - MOST) // span * span)
            part = slice(first, last)
            window = slice(low, last)
            q = queries[n, part]
            k = keys_in[n, window]
            v = values_in[n, window]
            g = grads_in[n, part]
            shape = (span, last - low)
            allowed = (col_ref[part] == row_ref[:, window]) & (
                lax.broadcasted_iota(jnp.int32, shape, 0) + first
                >= lax.broadcasted_iota(jnp.int32, shape, 1) + low
            )
            scores = jnp.where(allowed, cross_cols(q, k), -1e30)
            exps = jnp.exp(scores - jnp.max(scores, axis=-1, keepdims=True))
            probs = exps * (1.0 / jnp.sum(exps, axis=-1, keepdims=True))
            weights = probs.astype(bf16)
            out = jnp.dot(weights, v, preferred_element_type=f32).astype(bf16)
            mixed[n, part] = out
            delta = jnp.sum(g.astype(f32) * out.astype(f32), axis=-1, keepdims=True)
            grad_probs = cross_cols(g, v)
            grad_scores = (probs * (grad_probs - delta)).astype(bf16)
            grad_q[n, part] = jnp.dot(grad_scores, k, preferred_element_type=f32) * scale
            grad_k[n, window] += cross_rows(grad_scores, q)
            grad_v[n, window] += cross_rows(weights, g)
        return carry

    lax.fori_loop(0, heads, one_head, 0)

    sum_ref[...] = jnp.zeros_like(sum_ref)
    for first in range(0, length, span):
        part = slice(first, first + span)
        pieces = []
        for n in range(heads):
            both = jnp.concatenate([grad_q[n, part], grad_k[n, part]], axis=1)
            both = both * cos_ref[part] + turned(both * sin_ref[part], 1)
            pieces += [both, grad_v[n, part]]
        whole = jnp.concatenate(pieces, axis=1)
        sum_ref[...] += jnp.sum(whole, axis=0, keepdims=True)
        dx_ref[part] = whole.astype(bf16)
        o_ref[part] = jnp.concatenate([mixed[n, part] for n in range(heads)], axis=1)


def attention_branch(features, grad_rows, qkv_full, qkv_bias, out_full, segment_row):
    length = features.shape[0]
    heads = qkv_full.shape[1] // (3 * HEAD_DIM)
    cos_table, sin_table = rotary_tables(positions_of(segment_row))
    rest = ((0, 0), (0, HEAD_DIM - ROT))
    cos_full = jnp.tile(jnp.pad(cos_table, rest, constant_values=1.0), (1, 2))
    sin_full = jnp.tile(jnp.pad(sin_table, rest), (1, 2))
    half = ROT // 2
    source = jnp.arange(2 * HEAD_DIM)[:, None]
    target = jnp.arange(2 * HEAD_DIM)[None, :]
    inner = target % HEAD_DIM
    turn = jnp.where(
        (inner < half) & (source == target + half),
        -1.0,
        jnp.where((inner >= half) & (inner < ROT) & (source == target - half), 1.0, 0.0),
    ).astype(jnp.float32)
    wide = qkv_full.shape[1]
    vmem = pl.BlockSpec(memory_space=pltpu.VMEM)
    mixed_rows, packed_grad, sums = pl.pallas_call(
        functools.partial(attention_kernel, heads),
        out_shape=(
            jax.ShapeDtypeStruct((length, heads * HEAD_DIM), jnp.bfloat16),
            jax.ShapeDtypeStruct((length, wide), jnp.bfloat16),
            jax.ShapeDtypeStruct((1, wide), jnp.float32),
        ),
        in_specs=[vmem] * 10,
        out_specs=(vmem,) * 3,
        scratch_shapes=[pltpu.VMEM((heads, length, HEAD_DIM), jnp.bfloat16)] * 5
        + [pltpu.VMEM((heads, length, HEAD_DIM), jnp.float32)] * 3
        + [
            pltpu.VMEM((length, wide), jnp.float32),
            pltpu.VMEM((length, heads * HEAD_DIM), jnp.bfloat16),
        ],
        compiler_params=pltpu.CompilerParams(vmem_limit_bytes=56 * 1024 * 1024),
        name="attention",
    )(
        features,
        grad_rows,
        qkv_full,
        qkv_bias[None],
        out_full,
        cos_full,
        sin_full,
        turn,
        segment_row[:, None],
        segment_row[None, :],
    )
    return mixed_rows, packed_grad, sums[0]


def staged_body(
    layer_input,
    out_cotangent,
    segments,
    norm_gain,
    norm_bias,
    qkv_weight,
    qkv_bias,
    out_weight,
    out_bias,
    up_weight,
    up_bias,
    down_weight,
    down_bias,
):
    width_qkv = qkv_weight.shape[1]
    width_out = out_weight.shape[0]
    width_up = up_weight.shape[1]
    own_rows = layer_input.astype(jnp.float32)
    normed, inverse, shifted = layer_norm(own_rows, norm_gain, norm_bias)
    w_all, features, grad_rows = gather_all(
        jnp.concatenate([up_weight, down_weight.T, qkv_weight, out_weight.T], axis=1),
        shifted.astype(jnp.bfloat16),
        out_cotangent,
    )
    ends = (width_up, 2 * width_up, 2 * width_up + width_qkv)
    full_up, full_down, full_qkv, full_out = jnp.split(w_all, ends, axis=1)

    pre_act = jnp.dot(features, full_up, preferred_element_type=jnp.float32) + up_bias
    gelu_rows = gelu_value(pre_act).astype(jnp.bfloat16)
    grad_pre = jnp.dot(grad_rows, full_down, preferred_element_type=jnp.float32) * gelu_slope(
        pre_act
    )
    pre_grads = grad_pre.astype(jnp.bfloat16)
    up_bias_part = jnp.sum(grad_pre, axis=0)
    mixed_rows, packed_bf, qkv_bias_part = attention_branch(
        features, grad_rows, full_qkv, qkv_bias, full_out, segments[0]
    )
    branch = cross_cols(mixed_rows, full_out) + cross_cols(gelu_rows, full_down)
    feature_grad = cross_cols(packed_bf, full_qkv) + cross_cols(pre_grads, full_up)
    grads = [
        cross_rows(features, pre_grads).astype(jnp.bfloat16),
        cross_rows(grad_rows, gelu_rows).astype(jnp.bfloat16),
        cross_rows(features, packed_bf).astype(jnp.bfloat16),
        cross_rows(grad_rows, mixed_rows).astype(jnp.bfloat16),
    ]
    cot_rows = out_cotangent.astype(jnp.float32)
    model = own_rows.shape[1]
    biases = jnp.concatenate([qkv_bias_part, up_bias_part])
    bias_rows = -(-biases.shape[0] // model)
    biases = jnp.pad(biases, (0, bias_rows * model - biases.shape[0])).reshape(bias_rows, model)
    vectors = jnp.concatenate(
        [
            jnp.zeros((2, model), jnp.float32),
            jnp.sum(cot_rows, axis=0)[None],
            jnp.zeros((5, model), jnp.float32),
            biases,
            jnp.zeros((-bias_rows % 8, model), jnp.float32),
        ]
    )
    up_grad, down_grad, qkv_grad, out_grad, branch, row_grad, sums = scatter_all(
        grads,
        branch.astype(jnp.bfloat16),
        feature_grad.astype(jnp.bfloat16),
        normed,
        vectors,
    )
    layer_output = (own_rows + branch + out_bias + down_bias).astype(jnp.bfloat16)
    gain_grad, shift_grad, bias_grad = sums[0], sums[1], sums[2]
    bias_flat = sums[8 : 8 + bias_rows].reshape(-1)
    qkv_bias_grad = bias_flat[:width_qkv]
    up_bias_grad = bias_flat[width_qkv : width_qkv + width_up]
    scaled = row_grad * norm_gain
    input_grad = (
        cot_rows
        + inverse
        * (
            scaled
            - jnp.mean(scaled, axis=-1, keepdims=True)
            - normed * jnp.mean(scaled * normed, axis=-1, keepdims=True)
        )
    ).astype(jnp.bfloat16)
    return (
        layer_output,
        input_grad,
        gain_grad,
        shift_grad,
        qkv_grad,
        qkv_bias_grad,
        out_grad.T,
        bias_grad,
        up_grad,
        up_bias_grad,
        down_grad.T,
        bias_grad,
    )


DOCS = 4


def error_function(value):
    x = jnp.clip(value, -3.7439211627767994, 3.7439211627767994)
    y = x * x
    top = jnp.float32(0.00022905065861350646)
    for c in (
        0.0034082910107109506,
        0.050955695062380861,
        0.18520832239976145,
        1.128379143519084,
    ):
        top = top * y + jnp.float32(c)
    low = jnp.float32(-1.1791602954361697e-7)
    for c in (
        0.000023547966471313185,
        0.0010179625278914885,
        0.014070470171167667,
        0.11098505178285362,
        0.49746925110067538,
        1.0,
    ):
        low = low * y + jnp.float32(c)
    return x * top / low


def layer_kernel(
    fsdp,
    tp,
    heads,
    x_ref,
    c_ref,
    seg_ref,
    gain_ref,
    shift_ref,
    ob_ref,
    db_ref,
    bq_ref,
    bu_ref,
    wq_ref,
    wo_ref,
    wu_ref,
    wd_ref,
    y_out,
    dx_out,
    gq_out,
    go_out,
    gu_out,
    gd_out,
    v_out,
    w_all,
    h_all,
    c_all,
    h_turn,
    c_turn,
    normed_ref,
    inverse_ref,
    cos_ref,
    sin_a,
    sin_b,
    start_ref,
    qkv_ref,
    do_ref,
    queries,
    keys_in,
    values_in,
    grads_in,
    mixed,
    grad_q,
    grad_k,
    grad_v,
    o_ref,
    packed,
    gelu_ref,
    pre_ref,
    g_all,
    halves,
    joined,
    lands,
    part,
    mates,
    summed,
    sides_in,
    d_out,
    early,
    early_all,
    rows,
    rows_all,
    shared,
    up_send,
    down_send,
    z_recv,
    y_send,
    y_recv,
    x_send,
    x_recv,
    m_send,
    m_recv,
    a_send,
    a_recv,
    l_send,
    l_recv,
    pm_send,
    pm_recv,
    px_send,
    px_recv,
    e_send,
    e_recv,
    v_send,
    v_recv,
    u_send,
    u_recv,
):
    f32 = jnp.float32
    bf16 = jnp.bfloat16
    f, t, pair, line = place(fsdp, tp)
    lines = fsdp // 2
    sides = tp // 2
    side = lax.div(t, 2)
    par = lax.rem(t, 2)
    partner = 2 * line + 1 - pair
    mate = 2 * side + 1 - par
    block = x_ref.shape[0]
    model = x_ref.shape[1]
    shard = wu_ref.shape[0]
    hidden = wu_ref.shape[1]
    wide = wq_ref.shape[1]
    length = tp * block
    two = 2 * HEAD_DIM
    scale = HEAD_DIM ** (-0.5)
    half = ROT // 2

    barrier = pltpu.get_barrier_semaphore()
    each(
        1,
        fsdp,
        lambda step: pl.semaphore_signal(
            barrier, inc=1, device_id=(lax.rem(f + step, fsdp), t), device_id_type=MESH
        ),
    )
    each(
        1,
        tp,
        lambda step: pl.semaphore_signal(
            barrier, inc=1, device_id=(f, lax.rem(t + step, tp)), device_id_type=MESH
        ),
    )
    w_all[0, f] = jnp.concatenate([wq_ref[...], wo_ref[...].T], axis=1)
    w_all[1, f] = wu_ref[...]
    w_all[2, f] = wd_ref[...]
    c_all[t] = c_ref[...]
    own = x_ref[...].astype(f32)
    normed, inverse, shifted = layer_norm(own, gain_ref[...][None], shift_ref[...][None])
    h_all[t] = shifted.astype(bf16)
    normed_ref[...] = normed
    inverse_ref[...] = inverse
    pl.semaphore_wait(barrier, fsdp + tp - 2)

    def slot(origin):
        return 2 * origin + pair

    def z_copy(i, origin, send, to):
        view = w_all.at[i, slot(origin)]
        return remote(view, view, send.at[i, origin], z_recv.at[i, origin], (2 * to + pair, t))

    def z_up(i, origin):
        return z_copy(i, origin, up_send, line + 1)

    def z_down(i, origin):
        return z_copy(i, origin, down_send, line - 1)

    def y_copy(i, origin, side_of):
        view = w_all.at[i, 2 * origin + side_of]
        return remote(view, view, y_send.at[i, origin], y_recv.at[i, origin], (partner, t))

    def send_own(i):
        @pl.when(line + 1 < lines)
        def _():
            z_up(i, line).start()

        @pl.when(line > 0)
        def _():
            z_down(i, line).start()

        y_copy(i, line, pair).start()

    def relay(r):
        i = lax.div(r, lines - 1)
        k = lax.rem(r, lines - 1) + 1
        below = line - k
        above = line + k

        @pl.when(below >= 0)
        def _():
            z_up(i, below).wait_recv()

            @pl.when(line + 1 < lines)
            def _():
                z_up(i, below).start()

            y_copy(i, below, pair).start()

        @pl.when(above < lines)
        def _():
            z_down(i, above).wait_recv()

            @pl.when(line > 0)
            def _():
                z_down(i, above).start()

            y_copy(i, above, pair).start()

    relays = 3 * (lines - 1)

    tokens = (h_all, c_all)

    def x_copy(which, step, place_of):
        view = tokens[which].at[place_of]
        other = lax.rem(side + step, sides)
        return remote(
            view, view, x_send.at[which, step], x_recv.at[which, step], (f, 2 * other + par)
        )

    def m_copy(which, origin, parity):
        view = tokens[which].at[2 * origin + parity]
        return remote(
            view, view, m_send.at[which, origin], m_recv.at[which, origin], (f, mate)
        )

    def arrive(which):
        def one(step):
            origin = lax.rem(side + sides - step, sides)
            x_copy(which, step, 2 * origin + par).wait_recv()
            m_copy(which, origin, par).start()

        each(1, sides, one)

    def settle(which):
        each(0, sides, lambda origin: m_copy(which, origin, 1 - par).wait_recv())

    each(1, sides, lambda step: x_copy(0, step, t).start())
    send_own(0)
    m_copy(0, side, par).start()
    each(1, sides, lambda step: x_copy(1, step, t).start())
    m_copy(1, side, par).start()
    send_own(1)

    seg = seg_ref[...]
    down_rows = lax.broadcasted_iota(jnp.int32, (length, 1), 0)
    along_row = lax.broadcasted_iota(jnp.int32, (1, length), 1)
    start_col = jnp.zeros((length, 1), jnp.int32)
    start_row = jnp.zeros((1, length), jnp.int32)
    for d in range(1, DOCS):
        count = jnp.sum((seg < d).astype(jnp.int32), axis=1, keepdims=True)
        start_col = jnp.where(down_rows >= count, count, start_col)
        start_row = jnp.where(along_row >= count, count, start_row)
    start_ref[...] = start_col
    spot = (along_row - start_row).astype(f32)
    order = lax.broadcasted_iota(jnp.int32, (half, 1), 0).astype(f32)
    rates = jnp.exp(order * (-2.0 / ROT * 9.210340371976184))
    angles = spot * rates
    lane = lax.broadcasted_iota(jnp.int32, (half, two), 1) % HEAD_DIM
    pick = lax.broadcasted_iota(jnp.int32, (half, two), 0)
    first_half = (lane == pick).astype(f32)
    last_half = (lane == pick + half).astype(f32)

    def spread_out(table, matrix):
        return lax.dot_general(
            table,
            matrix,
            (((0,), (0,)), ((), ())),
            precision=lax.Precision.HIGHEST,
            preferred_element_type=f32,
        )

    cosine = jnp.cos(angles)
    sine = jnp.sin(angles)
    beyond = lax.broadcasted_iota(jnp.int32, (1, two), 1) % HEAD_DIM >= ROT
    cos_ref[...] = jnp.where(beyond, 1.0, spread_out(cosine, first_half + last_half))
    sin_a[...] = spread_out(sine, last_half)
    sin_b[...] = -spread_out(sine, first_half)

    each(0, lines - 1, relay)
    send_own(2)
    arrive(0)
    ahead_of = (lines - 1) + min(2, lines - 1)
    relay(lines - 1)
    settle(0)
    for s in range(tp):
        h_turn[:, s * block : (s + 1) * block] = h_all[s].T
    each(lines, ahead_of, relay)
    each(0, lines, lambda origin: y_copy(0, origin, 1 - pair).wait_recv())

    def project_q(s, carry):
        weight = w_all[0].reshape(model, model)
        part_of = pl.ds(s * block, block)
        qkv_ref[part_of] = (
            jnp.dot(h_all[s], weight[:, :wide], preferred_element_type=f32) + bq_ref[...][None]
        )
        return carry

    lax.fori_loop(0, tp, project_q, 0)
    arrive(1)

    def rotated(value, spots, sign):
        return (
            value * cos_ref[spots]
            + sign
            * (
                pltpu.roll(value, half, 1) * sin_a[spots]
                + pltpu.roll(value, two - half, 1) * sin_b[spots]
            )
        )

    for n in range(heads):
        base = 3 * HEAD_DIM * n

        def prepare(s, carry, n=n, base=base):
            spots = pl.ds(s * block, block)
            both = rotated(qkv_ref[spots, base : base + two], spots, 1.0)
            queries[n, spots] = both[:, :HEAD_DIM].astype(bf16) * bf16(scale)
            keys_in[n, spots] = both[:, HEAD_DIM:].astype(bf16)
            values_in[n, spots] = qkv_ref[spots, base + two : base + two + HEAD_DIM].astype(bf16)
            return carry

        lax.fori_loop(0, tp, prepare, 0)
    settle(1)
    for s in range(tp):
        c_turn[:, s * block : (s + 1) * block] = c_all[s].T

    def project_o(s, carry):
        weight = w_all[0].reshape(model, model)
        spots = pl.ds(s * block, block)
        value = jnp.dot(c_all[s], weight[:, wide:], preferred_element_type=f32).astype(bf16)
        for n in range(heads):
            grads_in[n, spots] = value[:, n * HEAD_DIM : (n + 1) * HEAD_DIM]
        return carry

    lax.fori_loop(0, tp, project_o, 0)
    grad_k[...] = jnp.zeros_like(grad_k)
    grad_v[...] = jnp.zeros_like(grad_v)
    span = min(SPAN, length)
    parts = length // span
    steps = heads * parts
    busy = max(1, steps * 3 // 4)
    left = relays - ahead_of

    def due(j):
        return ahead_of + jnp.minimum(left, lax.div(j * left, busy))

    def one_head(n, carry):
        for m in range(parts):
            first = m * span
            last = first + span
            low = max(0, (first - MOST) // span * span)
            spots = slice(first, last)
            window = slice(low, last)
            q = queries[n, spots]
            k = keys_in[n, window]
            v = values_in[n, window]
            g = grads_in[n, spots]
            shape = (span, last - low)
            key_at = lax.broadcasted_iota(jnp.int32, shape, 1) + low
            allowed = (key_at >= start_ref[spots]) & (
                lax.broadcasted_iota(jnp.int32, shape, 0) + first >= key_at
            )
            scores = jnp.where(allowed, cross_cols(q, k), -1e30)
            exps = jnp.exp(scores - jnp.max(scores, axis=-1, keepdims=True))
            probs = exps * (1.0 / jnp.sum(exps, axis=-1, keepdims=True))
            weights = probs.astype(bf16)
            out = jnp.dot(weights, v, preferred_element_type=f32).astype(bf16)
            mixed[n, spots] = out
            delta = jnp.sum(g.astype(f32) * out.astype(f32), axis=-1, keepdims=True)
            grad_probs = cross_cols(g, v)
            grad_scores = (probs * (grad_probs - delta)).astype(bf16)
            grad_q[n, spots] = jnp.dot(grad_scores, k, preferred_element_type=f32) * scale
            grad_k[n, window] += cross_rows(grad_scores, q)
            grad_v[n, window] += cross_rows(weights, g)
            j = n * parts + m
            each(due(j), due(j + 1), relay)
        return carry

    lax.fori_loop(0, heads, one_head, 0)

    early[...] = jnp.zeros_like(early)

    def finish(s, carry):
        spots = pl.ds(s * block, block)
        pieces = []
        for n in range(heads):
            both = jnp.concatenate([grad_q[n, spots], grad_k[n, spots]], axis=1)
            pieces += [rotated(both, spots, -1.0), grad_v[n, spots]]
        whole = jnp.concatenate(pieces, axis=1)
        early[0:1, :wide] += jnp.sum(whole, axis=0, keepdims=True)
        packed[spots] = whole.astype(bf16)
        o_ref[spots] = jnp.concatenate([mixed[n, spots] for n in range(heads)], axis=1)
        return carry

    lax.fori_loop(0, tp, finish, 0)

    def ahead(step):
        return lax.rem(line + step, lines)

    def across(i, step):
        return remote(
            g_all.at[i, 2 * ahead(step) + 1 - pair],
            halves.at[i, step],
            a_send.at[i, step],
            a_recv.at[i, step],
            (partner, t),
        )

    def along(i, step):
        return remote(
            joined.at[i, step],
            lands.at[i, step],
            l_send.at[i, step],
            l_recv.at[i, step],
            (2 * ahead(step) + pair, t),
        )

    def start_across(i):
        each(1, lines, lambda step: across(i, step).start())
        across(i, 0).start()

    def join(i, step):
        across(i, step).wait_recv()
        joined[i, step] = (
            g_all[i, 2 * ahead(step) + pair].astype(f32) + halves[i, step].astype(f32)
        ).astype(bf16)
        along(i, step).start()

    tile = model // 2
    many = tile // shard

    def store_grad(i, j, value):
        g_all[i, pl.ds(j * many, many)] = value.astype(bf16).reshape(many, shard, value.shape[1])

    def grad_attention(j, carry):
        spots = pl.ds(j * tile, tile)
        store_grad(
            0,
            j,
            jnp.concatenate(
                [
                    jnp.dot(h_turn[spots], packed[...], preferred_element_type=f32),
                    jnp.dot(c_turn[spots], o_ref[...], preferred_element_type=f32),
                ],
                axis=1,
            ),
        )
        return carry

    def grad_up(j, carry):
        store_grad(
            1,
            j,
            jnp.dot(h_turn[pl.ds(j * tile, tile)], pre_ref[...], preferred_element_type=f32),
        )
        return carry

    def grad_down(j, carry):
        store_grad(
            2,
            j,
            jnp.dot(c_turn[pl.ds(j * tile, tile)], gelu_ref[...], preferred_element_type=f32),
        )
        return carry

    lax.fori_loop(0, 2, grad_attention, 0)
    start_across(0)

    each(due(steps), relays, relay)
    each(0, lines, lambda origin: y_copy(1, origin, 1 - pair).wait_recv())
    each(0, lines, lambda origin: y_copy(2, origin, 1 - pair).wait_recv())

    def hidden_rows(s, carry):
        spots = pl.ds(s * block, block)
        up = w_all[1].reshape(model, hidden)
        down = w_all[2].reshape(model, hidden)
        a = jnp.dot(h_all[s], up, preferred_element_type=f32) + bu_ref[...][None]
        bell = 0.5 * (1.0 + error_function(a * 0.7071067811865476))
        gelu_ref[spots] = (a * bell).astype(bf16)
        slope = bell + a * jnp.exp(-0.5 * a * a) * 0.3989422804014327
        grad = jnp.dot(c_all[s], down, preferred_element_type=f32) * slope
        early[1:2, :hidden] += jnp.sum(grad, axis=0, keepdims=True)
        pre_ref[spots] = grad.astype(bf16)
        return carry

    lax.fori_loop(0, tp, hidden_rows, 0)

    def e_copy(step, place_of):
        return remote(
            early,
            early_all.at[place_of],
            e_send.at[step],
            e_recv.at[step],
            (lax.rem(f + step, fsdp), t),
        )

    early[2:3] = jnp.sum(c_all[t].astype(f32), axis=0, keepdims=True)
    join(0, 1)
    lax.fori_loop(0, 2, grad_up, 0)
    start_across(1)
    each(1, fsdp, lambda step: e_copy(step, f).start())
    join(0, 2)

    def pm_copy(which, origin):
        return remote(
            part.at[which, 2 * origin + 1 - par],
            mates.at[which, origin],
            pm_send.at[which, origin],
            pm_recv.at[which, origin],
            (f, mate),
        )

    def px_copy(which, step):
        other = lax.rem(side + step, sides)
        return remote(
            summed.at[which, step],
            sides_in.at[which, step],
            px_send.at[which, step],
            px_recv.at[which, step],
            (f, 2 * other + par),
        )

    def feature_rows(s, carry):
        spots = pl.ds(s * block, block)
        weight = w_all[0].reshape(model, model)
        part[0, s] = (
            cross_cols(packed[spots], weight[:, :wide])
            + cross_cols(pre_ref[spots], w_all[1].reshape(model, hidden))
        ).astype(bf16)
        return carry

    def branch_rows(s, carry):
        spots = pl.ds(s * block, block)
        weight = w_all[0].reshape(model, model)
        part[1, s] = (
            cross_cols(o_ref[spots], weight[:, wide:])
            + cross_cols(gelu_ref[spots], w_all[2].reshape(model, hidden))
        ).astype(bf16)
        return carry

    def pass_on(which):
        def one(step):
            other = lax.rem(side + step, sides)
            pm_copy(which, other).wait_recv()
            summed[which, step] = (
                part[which, 2 * other + par].astype(f32) + mates[which, other].astype(f32)
            ).astype(bf16)
            px_copy(which, step).start()

        each(1, sides, one)

    def gathered(which):
        pm_copy(which, side).wait_recv()
        d_out[...] = part[which, t].astype(f32) + mates[which, side].astype(f32)

        def one(step):
            px_copy(which, step).wait_recv()
            d_out[...] += sides_in[which, step].astype(f32)

        each(1, sides, one)

    lax.fori_loop(0, tp, feature_rows, 0)
    each(0, sides, lambda origin: pm_copy(0, origin).start())
    each(3, lines, lambda step: join(0, step))
    lax.fori_loop(0, 2, grad_down, 0)
    start_across(2)
    pass_on(0)
    lax.fori_loop(0, tp, branch_rows, 0)
    each(0, sides, lambda origin: pm_copy(1, origin).start())
    join(1, 1)
    pass_on(1)
    each(2, lines, lambda step: join(1, step))

    gathered(0)
    rows[...] = jnp.zeros_like(rows)
    rows[0:1] = jnp.sum(d_out[...] * normed_ref[...], axis=0, keepdims=True)
    rows[1:2] = jnp.sum(d_out[...], axis=0, keepdims=True)
    each(1, fsdp, lambda step: e_copy(step, lax.rem(f + fsdp - step, fsdp)).wait_recv())
    early_all[f] = early[...]
    total = lax.fori_loop(1, fsdp, lambda step, value: value + early_all[step], early_all[0])
    v_out[8:16] = total
    rows[2:3] = early[2:3]

    def v_copy(step, place_of):
        return remote(
            rows,
            rows_all.at[place_of],
            v_send.at[step],
            v_recv.at[step],
            (lax.rem(f + step, fsdp), t),
        )

    each(1, fsdp, lambda step: v_copy(step, f).start())
    rows_all[f] = rows[...]
    normed = normed_ref[...]
    scaled = d_out[...] * gain_ref[...][None]
    dx_out[...] = (
        c_ref[...].astype(f32)
        + inverse_ref[...]
        * (
            scaled
            - jnp.mean(scaled, axis=-1, keepdims=True)
            - normed * jnp.mean(scaled * normed, axis=-1, keepdims=True)
        )
    ).astype(bf16)
    join(2, 1)
    each(1, fsdp, lambda step: v_copy(step, lax.rem(f + fsdp - step, fsdp)).wait_recv())
    shared[t] = lax.fori_loop(1, fsdp, lambda step, value: value + rows_all[step], rows_all[0])

    def u_copy(step, place_of):
        view = shared.at[place_of]
        return remote(
            shared.at[t],
            view,
            u_send.at[step],
            u_recv.at[step],
            (f, lax.rem(t + step, tp)),
        )

    each(1, tp, lambda step: u_copy(step, t).start())
    each(2, lines, lambda step: join(2, step))
    gathered(1)
    y_out[...] = (
        x_ref[...].astype(f32) + d_out[...] + ob_ref[...][None] + db_ref[...][None]
    ).astype(bf16)
    each(1, tp, lambda step: u_copy(step, lax.rem(t + tp - step, tp)).wait_recv())
    whole = shared[0]
    for step in range(1, tp):
        whole = whole + shared[step]
    v_out[0:8] = whole

    def collected(i):
        across(i, 0).wait_recv()
        value = g_all[i, f].astype(f32) + halves[i, 0].astype(f32)

        def one(step, value):
            along(i, step).wait_recv()
            return value + lands[i, step].astype(f32)

        return lax.fori_loop(1, lines, one, value)

    value = collected(0)
    gq_out[...] = value[:, :wide]
    go_out[...] = value[:, wide:]
    gu_out[...] = collected(1)
    gd_out[...] = collected(2)

    for i in range(3):

        @pl.when(line + 1 < lines)
        def _():
            each(0, line + 1, lambda origin: z_up(i, origin).wait_send())

        @pl.when(line > 0)
        def _():
            each(line, lines, lambda origin: z_down(i, origin).wait_send())

        each(0, lines, lambda origin: y_copy(i, origin, pair).wait_send())
        each(0, lines, lambda step: across(i, step).wait_send())
        each(1, lines, lambda step: along(i, step).wait_send())
    for which in range(2):
        each(1, sides, lambda step: x_copy(which, step, t).wait_send())
        each(0, sides, lambda origin: m_copy(which, origin, par).wait_send())
        each(0, sides, lambda origin: pm_copy(which, origin).wait_send())
        each(1, sides, lambda step: px_copy(which, step).wait_send())
    each(1, fsdp, lambda step: e_copy(step, f).wait_send())
    each(1, fsdp, lambda step: v_copy(step, f).wait_send())
    each(1, tp, lambda step: u_copy(step, t).wait_send())


def layer_call(x, c, seg, gain, shift, ob, db, bq, bu, wq, wo, wu, wd):
    fsdp = lax.axis_size("fsdp")
    tp = lax.axis_size("tp")
    lines = fsdp // 2
    sides = tp // 2
    block, model = x.shape
    shard, hidden = wu.shape
    wide = wq.shape[1]
    heads = wide // (3 * HEAD_DIM)
    length = tp * block
    two = 2 * HEAD_DIM
    f32 = jnp.float32
    bf16 = jnp.bfloat16
    vmem = pl.BlockSpec(memory_space=pltpu.VMEM)
    dma = pltpu.SemaphoreType.DMA
    buf = pltpu.VMEM
    return pl.pallas_call(
        functools.partial(layer_kernel, fsdp, tp, heads),
        out_shape=(
            jax.ShapeDtypeStruct((block, model), bf16),
            jax.ShapeDtypeStruct((block, model), bf16),
            jax.ShapeDtypeStruct((shard, wide), f32),
            jax.ShapeDtypeStruct((shard, model - wide), f32),
            jax.ShapeDtypeStruct((shard, hidden), f32),
            jax.ShapeDtypeStruct((shard, hidden), f32),
            jax.ShapeDtypeStruct((16, model), f32),
        ),
        in_specs=[vmem] * 13,
        out_specs=(vmem,) * 7,
        scratch_shapes=[
            buf((3, fsdp, shard, model), bf16),
            buf((tp, block, model), bf16),
            buf((tp, block, model), bf16),
            buf((model, length), bf16),
            buf((model, length), bf16),
            buf((block, model), f32),
            buf((block, 1), f32),
            buf((length, two), f32),
            buf((length, two), f32),
            buf((length, two), f32),
            buf((length, 1), jnp.int32),
            buf((length, wide), f32),
            buf((8, 128), f32),
        ]
        + [buf((heads, length, HEAD_DIM), bf16)] * 5
        + [buf((heads, length, HEAD_DIM), f32)] * 3
        + [
            buf((length, heads * HEAD_DIM), bf16),
            buf((length, wide), bf16),
            buf((length, hidden), bf16),
            buf((length, hidden), bf16),
            buf((3, fsdp, shard, model), bf16),
            buf((3, lines, shard, model), bf16),
            buf((3, lines, shard, model), bf16),
            buf((3, lines, shard, model), bf16),
            buf((2, tp, block, model), bf16),
            buf((2, sides, block, model), bf16),
            buf((2, sides, block, model), bf16),
            buf((2, sides, block, model), bf16),
            buf((block, model), f32),
            buf((8, model), f32),
            buf((fsdp, 8, model), f32),
            buf((8, model), f32),
            buf((fsdp, 8, model), f32),
            buf((tp, 8, model), f32),
        ]
        + [dma((3, lines))] * 5
        + [dma((2, sides))] * 4
        + [dma((3, lines))] * 4
        + [dma((2, sides))] * 4
        + [dma((fsdp,))] * 4
        + [dma((tp,))] * 2,
        compiler_params=pltpu.CompilerParams(
            collective_id=3, has_side_effects=True, vmem_limit_bytes=62 * 1024 * 1024
        ),
        name="layer",
    )(x, c, seg, gain, shift, ob, db, bq, bu, wq, wo, wu, wd)


def deliver_kernel(y, dx, gq, go, gu, gd, v, *refs):
    outs, (turned, sums, sems) = refs[:12], refs[12:]
    pairs = (
        (v, sums),
        (go, turned),
        (y, outs[0]),
        (dx, outs[1]),
        (gq, outs[4]),
        (gu, outs[8]),
        (gd, outs[10]),
    )
    copies = [
        pltpu.make_async_copy(source, target, sems.at[i])
        for i, (source, target) in enumerate(pairs)
    ]
    for copy in copies:
        copy.start()
    copies[0].wait()
    for place_of, row in ((2, 0), (3, 1), (5, 8), (7, 2), (9, 9), (11, 2)):
        outs[place_of][...] = sums[row][: outs[place_of].shape[0]]
    copies[1].wait()
    outs[6][...] = turned[...].T
    for copy in copies[2:]:
        copy.wait()


def deliver(y, dx, gq, go, gu, gd, v):
    f32 = jnp.float32
    vmem = pl.BlockSpec(memory_space=pltpu.VMEM)
    line = jax.ShapeDtypeStruct((y.shape[1],), f32)
    return pl.pallas_call(
        deliver_kernel,
        out_shape=(
            jax.ShapeDtypeStruct(y.shape, y.dtype),
            jax.ShapeDtypeStruct(dx.shape, dx.dtype),
            line,
            line,
            jax.ShapeDtypeStruct(gq.shape, f32),
            jax.ShapeDtypeStruct((gq.shape[1],), f32),
            jax.ShapeDtypeStruct((go.shape[1], go.shape[0]), f32),
            line,
            jax.ShapeDtypeStruct(gu.shape, f32),
            jax.ShapeDtypeStruct((gu.shape[1],), f32),
            jax.ShapeDtypeStruct(gd.shape, f32),
            line,
        ),
        in_specs=[pl.BlockSpec(memory_space=pl.ANY)] * 7,
        out_specs=(vmem,) * 12,
        scratch_shapes=[
            pltpu.VMEM(go.shape, f32),
            pltpu.VMEM(v.shape, f32),
            pltpu.SemaphoreType.DMA((7,)),
        ],
        compiler_params=pltpu.CompilerParams(vmem_limit_bytes=60 * 1024 * 1024),
        name="deliver",
    )(y, dx, gq, go, gu, gd, v)


def fused_body(
    layer_input,
    out_cotangent,
    segments,
    norm_gain,
    norm_bias,
    qkv_weight,
    qkv_bias,
    out_weight,
    out_bias,
    up_weight,
    up_bias,
    down_weight,
    down_bias,
):
    y, dx, qkv_grad, out_grad, up_grad, down_grad, sums = layer_call(
        layer_input,
        out_cotangent,
        segments,
        norm_gain,
        norm_bias,
        out_bias,
        down_bias,
        qkv_bias,
        up_bias,
        qkv_weight,
        out_weight,
        up_weight,
        down_weight.T,
    )
    outs = list(deliver(y, dx, qkv_grad, out_grad, up_grad, down_grad, sums))
    outs[10] = outs[10].T
    return tuple(outs)


def body(*args):
    rows = args[5].shape[0]
    model, hidden = args[9].shape[0] * lax.axis_size("fsdp"), args[9].shape[1]
    fits = (
        rows % 16 == 0
        and (model // 2) % rows == 0
        and args[5].shape[1] + args[7].shape[0] == model == hidden
        and args[2].shape == (1, lax.axis_size("tp") * args[0].shape[0])
        and args[0].shape[0] == SPAN
    )
    return fused_body(*args) if fits else staged_body(*args)


def solution(mesh):
    in_specs = (
        P(("fsdp", "tp"), None),
        P(("fsdp", "tp"), None),
        P("fsdp", None),
        P(),
        P(),
        P("fsdp", "tp"),
        P("tp"),
        P("tp", "fsdp"),
        P(),
        P("fsdp", "tp"),
        P("tp"),
        P("tp", "fsdp"),
        P(),
    )
    out_specs = (
        P(("fsdp", "tp"), None),
        P(("fsdp", "tp"), None),
        P(),
        P(),
        P("fsdp", "tp"),
        P("tp"),
        P("tp", "fsdp"),
        P(),
        P("fsdp", "tp"),
        P("tp"),
        P("tp", "fsdp"),
        P(),
    )
    return jax.shard_map(body, mesh=mesh, in_specs=in_specs, out_specs=out_specs, check_vma=False)
```

```python
import functools

import jax
import jax.numpy as jnp
from jax import lax
from jax.experimental import pallas as pl
from jax.experimental.pallas import tpu as pltpu
from jax.sharding import PartitionSpec as P

HEAD_DIM = 64
ROT = 16


EPSILON = 1e-05
ROTARY_BASE = 10000.0


def layer_norm(values, gain, shift):
    center = values - jnp.mean(values, axis=-1, keepdims=True)
    spread = jnp.mean(center * center, axis=-1, keepdims=True)
    inverse = lax.rsqrt(spread + EPSILON)
    normed = center * inverse
    return (normed, inverse, normed * gain + shift)


def gelu_value(pre_act):
    return 0.5 * pre_act * (1.0 + lax.erf(pre_act * 0.7071067811865476))


def gelu_slope(pre_act):
    return (
        0.5 * (1.0 + lax.erf(pre_act * 0.7071067811865476))
        + pre_act * jnp.exp(-0.5 * pre_act * pre_act) * 0.3989422804014327
    )


def positions_of(segment_row):
    length = segment_row.shape[0]
    counter = jnp.arange(length, dtype=jnp.int32)
    is_start = jnp.concatenate(
        [jnp.ones((1,), dtype=jnp.bool_), segment_row[1:] != segment_row[:-1]]
    )
    starts = lax.cummax(jnp.where(is_start, counter, jnp.zeros_like(counter)), axis=0)
    return counter - starts


def rotary_tables(positions):
    halves = ROT // 2
    inverse_freq = ROTARY_BASE ** (-(jnp.arange(halves, dtype=jnp.float32) * 2.0) / ROT)
    angles = positions.astype(jnp.float32)[:, None] * inverse_freq[None, :]
    cos_table = jnp.cos(angles)
    sin_table = jnp.sin(angles)
    return (
        jnp.concatenate([cos_table, cos_table], axis=-1),
        jnp.concatenate([sin_table, sin_table], axis=-1),
    )


def cross_rows(left, right):
    return lax.dot_general(
        left, right, (((0,), (0,)), ((), ())), preferred_element_type=jnp.float32
    )


def cross_cols(left, right):
    return lax.dot_general(
        left, right, (((1,), (1,)), ((), ())), preferred_element_type=jnp.float32
    )


MESH = pl.DeviceIdType.MESH


def place(fsdp, tp):
    f = lax.axis_index("fsdp")
    t = lax.axis_index("tp")
    pair = lax.rem(f, 2)
    line = lax.div(f, 2)
    return f, t, pair, line


def remote(source, target, send, recv, device):
    return pltpu.make_async_remote_copy(
        src_ref=source,
        dst_ref=target,
        send_sem=send,
        recv_sem=recv,
        device_id=device,
        device_id_type=MESH,
    )


def each(first, last, action):
    def step_of(step, carry):
        action(step)
        return carry

    lax.fori_loop(first, last, step_of, 0)


def greet(fsdp, tp):
    f, t, _, _ = place(fsdp, tp)
    barrier = pltpu.get_barrier_semaphore()
    each(
        1,
        fsdp,
        lambda step: pl.semaphore_signal(
            barrier, inc=1, device_id=(lax.rem(f + step, fsdp), t), device_id_type=MESH
        ),
    )
    each(
        1,
        tp,
        lambda step: pl.semaphore_signal(
            barrier, inc=1, device_id=(f, lax.rem(t + step, tp)), device_id_type=MESH
        ),
    )
    pl.semaphore_wait(barrier, fsdp + tp - 2)


def gather_kernel(
    fsdp, tp, w_ref, h_ref, c_ref, w_out, h_out, c_out, w_send, w_recv, p_send, p_recv, r_send, r_recv
):
    f, t, pair, line = place(fsdp, tp)
    lines = fsdp // 2
    greet(fsdp, tp)
    partner = 2 * line + 1 - pair

    def along(step, slot):
        other = lax.rem(line + step, lines)
        return remote(
            w_ref, w_out.at[slot], w_send.at[step], w_recv.at[step], (2 * other + pair, t)
        )

    def across(step, source, slot):
        return remote(source, w_out.at[slot], p_send.at[step], p_recv.at[step], (partner, t))

    def beside(step, which, source, target, slot):
        return remote(
            source,
            target.at[slot],
            r_send.at[which, step],
            r_recv.at[which, step],
            (f, lax.rem(t + step, tp)),
        )

    def came(step, side):
        return 2 * lax.rem(line + lines - step, lines) + side

    across(0, w_ref, f).start()
    each(1, lines, lambda step: along(step, f).start())
    each(1, tp, lambda step: beside(step, 0, h_ref, h_out, t).start())
    each(1, tp, lambda step: beside(step, 1, c_ref, c_out, t).start())
    w_out[f] = w_ref[...]
    h_out[t] = h_ref[...]
    c_out[t] = c_ref[...]

    def forward(step):
        slot = came(step, pair)
        along(step, slot).wait_recv()
        across(step, w_out.at[slot], slot).start()

    each(1, lines, forward)

    def settle(step):
        slot = lax.rem(t + tp - step, tp)
        beside(step, 0, h_ref, h_out, slot).wait()
        beside(step, 1, c_ref, c_out, slot).wait()

    each(1, tp, settle)
    each(1, lines, lambda step: along(step, f).wait_send())

    def finish(step):
        across(step, w_ref, came(step, 1 - pair)).wait()

    each(0, lines, finish)


def gather_all(weights, features, cotangent):
    fsdp = lax.axis_size("fsdp")
    tp = lax.axis_size("tp")
    vmem = pl.BlockSpec(memory_space=pltpu.VMEM)
    shapes = (
        jax.ShapeDtypeStruct((fsdp,) + weights.shape, weights.dtype),
        jax.ShapeDtypeStruct((tp,) + features.shape, features.dtype),
        jax.ShapeDtypeStruct((tp,) + cotangent.shape, cotangent.dtype),
    )
    dma = pltpu.SemaphoreType.DMA
    w_all, h_all, c_all = pl.pallas_call(
        functools.partial(gather_kernel, fsdp, tp),
        out_shape=shapes,
        in_specs=[vmem] * 3,
        out_specs=(vmem,) * 3,
        scratch_shapes=[
            dma((fsdp // 2,)),
            dma((fsdp // 2,)),
            dma((fsdp // 2,)),
            dma((fsdp // 2,)),
            dma((2, tp)),
            dma((2, tp)),
        ],
        compiler_params=pltpu.CompilerParams(
            collective_id=1, has_side_effects=True, vmem_limit_bytes=48 * 1024 * 1024
        ),
        name="gather_all",
    )(weights, features, cotangent)
    return (
        w_all.reshape(fsdp * weights.shape[0], weights.shape[1]),
        h_all.reshape(tp * features.shape[0], features.shape[1]),
        c_all.reshape(tp * cotangent.shape[0], cotangent.shape[1]),
    )


def scatter_kernel(
    fsdp,
    tp,
    many,
    *refs,
):
    g_refs, refs = refs[:many], refs[many:]
    b_ref, d_ref, n_ref, v_ref = refs[:4]
    g_outs, refs = refs[4 : 4 + many], refs[4 + many :]
    b_out, d_out, v_out = refs[:3]
    halves, joined, lands = (refs[3 + many * i : 3 + many * (i + 1)] for i in range(3))
    (
        b_land,
        d_land,
        rows,
        first,
        second,
        p_send,
        p_recv,
        w_send,
        w_recv,
        r_send,
        r_recv,
        v_send,
        v_recv,
        u_send,
        u_recv,
    ) = refs[3 + 3 * many :]
    f, t, pair, line = place(fsdp, tp)
    lines = fsdp // 2
    greet(fsdp, tp)
    partner = 2 * line + 1 - pair

    def ahead(step):
        return lax.rem(line + step, lines)

    def across(i, step):
        return remote(
            g_refs[i].at[2 * ahead(step) + 1 - pair],
            halves[i].at[step],
            p_send.at[i, step],
            p_recv.at[i, step],
            (partner, t),
        )

    def along(i, step):
        return remote(
            joined[i].at[step],
            lands[i].at[step],
            w_send.at[i, step],
            w_recv.at[i, step],
            (2 * ahead(step) + pair, t),
        )

    def beside(step, which, source, target):
        return remote(
            source.at[lax.rem(t + step, tp)],
            target.at[step],
            r_send.at[which, step],
            r_recv.at[which, step],
            (f, lax.rem(t + step, tp)),
        )

    def start_beside(step):
        beside(step, 1, d_ref, d_land).start()
        beside(step, 0, b_ref, b_land).start()

    def start_across(step):
        for i in range(many):
            across(i, step).start()

    each(1, lines, start_across)
    start_across(0)
    each(1, tp, start_beside)

    def join(step):
        for i in range(many):
            across(i, step).wait_recv()
            joined[i][step] = (
                g_refs[i][2 * ahead(step) + pair].astype(jnp.float32)
                + halves[i][step].astype(jnp.float32)
            ).astype(joined[i].dtype)
            along(i, step).start()

    each(1, lines, join)
    for i in range(many):
        across(i, 0).wait_recv()
        g_outs[i][...] = g_refs[i][f].astype(jnp.float32) + halves[i][0].astype(jnp.float32)

    d_out[...] = d_ref[t].astype(jnp.float32)
    b_out[...] = b_ref[t].astype(jnp.float32)

    def gather_d(step):
        beside(step, 1, d_ref, d_land).wait()
        d_out[...] += d_land[step].astype(jnp.float32)

    def gather_b(step):
        beside(step, 0, b_ref, b_land).wait()
        b_out[...] += b_land[step].astype(jnp.float32)

    each(1, tp, gather_d)
    rows[...] = v_ref[...]
    rows[0:1] = jnp.sum(d_out[...] * n_ref[...], axis=0, keepdims=True)
    rows[1:2] = jnp.sum(d_out[...], axis=0, keepdims=True)

    def spread(step, slot):
        return remote(
            rows,
            first.at[slot],
            v_send.at[step],
            v_recv.at[step],
            (lax.rem(f + step, fsdp), t),
        )

    each(1, fsdp, lambda step: spread(step, f).start())
    first[f] = rows[...]
    each(1, tp, gather_b)

    def collect(step):
        for i in range(many):
            along(i, step).wait_recv()
            g_outs[i][...] += lands[i][step].astype(jnp.float32)

    each(1, lines, collect)
    each(1, fsdp, lambda step: spread(step, lax.rem(f + fsdp - step, fsdp)).wait())
    total = lax.fori_loop(1, fsdp, lambda step, value: value + first[step], first[0])
    second[t] = total[:8]
    v_out[...] = total

    def share(step, slot):
        return remote(
            second.at[t],
            second.at[slot],
            u_send.at[step],
            u_recv.at[step],
            (f, lax.rem(t + step, tp)),
        )

    each(1, tp, lambda step: share(step, t).start())

    def sent_along(step):
        for i in range(many):
            along(i, step).wait_send()

    def sent_across(step):
        for i in range(many):
            across(i, step).wait_send()

    each(1, lines, sent_along)
    each(0, lines, sent_across)
    each(1, tp, lambda step: share(step, lax.rem(t + tp - step, tp)).wait())
    whole = second[0]
    for step in range(1, tp):
        whole = whole + second[step]
    v_out[:8] = whole


def scatter_all(grads, branch, feature_grad, normed, vectors):
    fsdp = lax.axis_size("fsdp")
    tp = lax.axis_size("tp")
    lines = fsdp // 2
    grads = [grad.reshape(fsdp, -1, grad.shape[1]) for grad in grads]
    many = len(grads)
    branch = branch.reshape(tp, -1, branch.shape[1])
    feature_grad = feature_grad.reshape(tp, -1, feature_grad.shape[1])
    vmem = pl.BlockSpec(memory_space=pltpu.VMEM)
    dma = pltpu.SemaphoreType.DMA
    f32 = jnp.float32
    return pl.pallas_call(
        functools.partial(scatter_kernel, fsdp, tp, many),
        out_shape=(
            *(jax.ShapeDtypeStruct(grad.shape[1:], f32) for grad in grads),
            jax.ShapeDtypeStruct(branch.shape[1:], f32),
            jax.ShapeDtypeStruct(feature_grad.shape[1:], f32),
            jax.ShapeDtypeStruct(vectors.shape, f32),
        ),
        in_specs=[vmem] * (many + 4),
        out_specs=(vmem,) * (many + 3),
        scratch_shapes=[
            *(
                pltpu.VMEM((lines,) + grad.shape[1:], grad.dtype)
                for _ in range(3)
                for grad in grads
            ),
            pltpu.VMEM(branch.shape, branch.dtype),
            pltpu.VMEM(feature_grad.shape, feature_grad.dtype),
            pltpu.VMEM(vectors.shape, f32),
            pltpu.VMEM((fsdp,) + vectors.shape, f32),
            pltpu.VMEM((tp, 8, vectors.shape[1]), f32),
            dma((many, lines)),
            dma((many, lines)),
            dma((many, lines)),
            dma((many, lines)),
            dma((2, tp)),
            dma((2, tp)),
            dma((fsdp,)),
            dma((fsdp,)),
            dma((tp,)),
            dma((tp,)),
        ],
        compiler_params=pltpu.CompilerParams(
            collective_id=2, has_side_effects=True, vmem_limit_bytes=56 * 1024 * 1024
        ),
        name="scatter_all",
    )(*grads, branch, feature_grad, normed, vectors)


MOST = 512
SPAN = 256


def attention_kernel(
    heads,
    f_ref,
    c_ref,
    wq_ref,
    bq_ref,
    wo_ref,
    cos_ref,
    sin_ref,
    turn_ref,
    col_ref,
    row_ref,
    o_ref,
    dx_ref,
    sum_ref,
    queries,
    keys_in,
    values_in,
    grads_in,
    mixed,
    grad_q,
    grad_k,
    grad_v,
    x_ref,
    do_ref,
):
    length = f_ref.shape[0]
    span = min(SPAN, length)
    scale = HEAD_DIM ** (-0.5)
    two = 2 * HEAD_DIM
    f32 = jnp.float32
    bf16 = jnp.bfloat16

    def turned(value, axis):
        return lax.dot_general(
            value,
            turn_ref[...],
            (((1,), (axis,)), ((), ())),
            precision=lax.Precision.HIGHEST,
            preferred_element_type=f32,
        )

    for first in range(0, length, span):
        part = slice(first, first + span)
        x_ref[part] = (
            jnp.dot(f_ref[part], wq_ref[...], preferred_element_type=f32) + bq_ref[...]
        )
        do_ref[part] = jnp.dot(c_ref[part], wo_ref[...], preferred_element_type=f32).astype(bf16)
    for n in range(heads):
        base = 3 * HEAD_DIM * n
        for first in range(0, length, span):
            part = slice(first, first + span)
            both = x_ref[part, base : base + two]
            both = both * cos_ref[part] + turned(both, 0) * sin_ref[part]
            queries[n, part] = both[:, :HEAD_DIM].astype(bf16) * bf16(scale)
            keys_in[n, part] = both[:, HEAD_DIM:].astype(bf16)
            values_in[n, part] = x_ref[part, base + two : base + two + HEAD_DIM].astype(bf16)
            grads_in[n, part] = do_ref[part, n * HEAD_DIM : (n + 1) * HEAD_DIM]
    grad_k[...] = jnp.zeros_like(grad_k)
    grad_v[...] = jnp.zeros_like(grad_v)

    def one_head(n, carry):
        for first in range(0, length, span):
            last = first + span
            low = max(0, (first - MOST) // span * span)
            part = slice(first, last)
            window = slice(low, last)
            q = queries[n, part]
            k = keys_in[n, window]
            v = values_in[n, window]
            g = grads_in[n, part]
            shape = (span, last - low)
            allowed = (col_ref[part] == row_ref[:, window]) & (
                lax.broadcasted_iota(jnp.int32, shape, 0) + first
                >= lax.broadcasted_iota(jnp.int32, shape, 1) + low
            )
            scores = jnp.where(allowed, cross_cols(q, k), -1e30)
            exps = jnp.exp(scores - jnp.max(scores, axis=-1, keepdims=True))
            probs = exps * (1.0 / jnp.sum(exps, axis=-1, keepdims=True))
            weights = probs.astype(bf16)
            out = jnp.dot(weights, v, preferred_element_type=f32).astype(bf16)
            mixed[n, part] = out
            delta = jnp.sum(g.astype(f32) * out.astype(f32), axis=-1, keepdims=True)
            grad_probs = cross_cols(g, v)
            grad_scores = (probs * (grad_probs - delta)).astype(bf16)
            grad_q[n, part] = jnp.dot(grad_scores, k, preferred_element_type=f32) * scale
            grad_k[n, window] += cross_rows(grad_scores, q)
            grad_v[n, window] += cross_rows(weights, g)
        return carry

    lax.fori_loop(0, heads, one_head, 0)

    sum_ref[...] = jnp.zeros_like(sum_ref)
    for first in range(0, length, span):
        part = slice(first, first + span)
        pieces = []
        for n in range(heads):
            both = jnp.concatenate([grad_q[n, part], grad_k[n, part]], axis=1)
            both = both * cos_ref[part] + turned(both * sin_ref[part], 1)
            pieces += [both, grad_v[n, part]]
        whole = jnp.concatenate(pieces, axis=1)
        sum_ref[...] += jnp.sum(whole, axis=0, keepdims=True)
        dx_ref[part] = whole.astype(bf16)
        o_ref[part] = jnp.concatenate([mixed[n, part] for n in range(heads)], axis=1)


def attention_branch(features, grad_rows, qkv_full, qkv_bias, out_full, segment_row):
    length = features.shape[0]
    heads = qkv_full.shape[1] // (3 * HEAD_DIM)
    cos_table, sin_table = rotary_tables(positions_of(segment_row))
    rest = ((0, 0), (0, HEAD_DIM - ROT))
    cos_full = jnp.tile(jnp.pad(cos_table, rest, constant_values=1.0), (1, 2))
    sin_full = jnp.tile(jnp.pad(sin_table, rest), (1, 2))
    half = ROT // 2
    source = jnp.arange(2 * HEAD_DIM)[:, None]
    target = jnp.arange(2 * HEAD_DIM)[None, :]
    inner = target % HEAD_DIM
    turn = jnp.where(
        (inner < half) & (source == target + half),
        -1.0,
        jnp.where((inner >= half) & (inner < ROT) & (source == target - half), 1.0, 0.0),
    ).astype(jnp.float32)
    wide = qkv_full.shape[1]
    vmem = pl.BlockSpec(memory_space=pltpu.VMEM)
    mixed_rows, packed_grad, sums = pl.pallas_call(
        functools.partial(attention_kernel, heads),
        out_shape=(
            jax.ShapeDtypeStruct((length, heads * HEAD_DIM), jnp.bfloat16),
            jax.ShapeDtypeStruct((length, wide), jnp.bfloat16),
            jax.ShapeDtypeStruct((1, wide), jnp.float32),
        ),
        in_specs=[vmem] * 10,
        out_specs=(vmem,) * 3,
        scratch_shapes=[pltpu.VMEM((heads, length, HEAD_DIM), jnp.bfloat16)] * 5
        + [pltpu.VMEM((heads, length, HEAD_DIM), jnp.float32)] * 3
        + [
            pltpu.VMEM((length, wide), jnp.float32),
            pltpu.VMEM((length, heads * HEAD_DIM), jnp.bfloat16),
        ],
        compiler_params=pltpu.CompilerParams(vmem_limit_bytes=56 * 1024 * 1024),
        name="attention",
    )(
        features,
        grad_rows,
        qkv_full,
        qkv_bias[None],
        out_full,
        cos_full,
        sin_full,
        turn,
        segment_row[:, None],
        segment_row[None, :],
    )
    return mixed_rows, packed_grad, sums[0]


def staged_body(
    layer_input,
    out_cotangent,
    segments,
    norm_gain,
    norm_bias,
    qkv_weight,
    qkv_bias,
    out_weight,
    out_bias,
    up_weight,
    up_bias,
    down_weight,
    down_bias,
):
    width_qkv = qkv_weight.shape[1]
    width_out = out_weight.shape[0]
    width_up = up_weight.shape[1]
    own_rows = layer_input.astype(jnp.float32)
    normed, inverse, shifted = layer_norm(own_rows, norm_gain, norm_bias)
    w_all, features, grad_rows = gather_all(
        jnp.concatenate([up_weight, down_weight.T, qkv_weight, out_weight.T], axis=1),
        shifted.astype(jnp.bfloat16),
        out_cotangent,
    )
    ends = (width_up, 2 * width_up, 2 * width_up + width_qkv)
    full_up, full_down, full_qkv, full_out = jnp.split(w_all, ends, axis=1)

    pre_act = jnp.dot(features, full_up, preferred_element_type=jnp.float32) + up_bias
    gelu_rows = gelu_value(pre_act).astype(jnp.bfloat16)
    grad_pre = jnp.dot(grad_rows, full_down, preferred_element_type=jnp.float32) * gelu_slope(
        pre_act
    )
    pre_grads = grad_pre.astype(jnp.bfloat16)
    up_bias_part = jnp.sum(grad_pre, axis=0)
    mixed_rows, packed_bf, qkv_bias_part = attention_branch(
        features, grad_rows, full_qkv, qkv_bias, full_out, segments[0]
    )
    branch = cross_cols(mixed_rows, full_out) + cross_cols(gelu_rows, full_down)
    feature_grad = cross_cols(packed_bf, full_qkv) + cross_cols(pre_grads, full_up)
    grads = [
        cross_rows(features, pre_grads).astype(jnp.bfloat16),
        cross_rows(grad_rows, gelu_rows).astype(jnp.bfloat16),
        cross_rows(features, packed_bf).astype(jnp.bfloat16),
        cross_rows(grad_rows, mixed_rows).astype(jnp.bfloat16),
    ]
    cot_rows = out_cotangent.astype(jnp.float32)
    model = own_rows.shape[1]
    biases = jnp.concatenate([qkv_bias_part, up_bias_part])
    bias_rows = -(-biases.shape[0] // model)
    biases = jnp.pad(biases, (0, bias_rows * model - biases.shape[0])).reshape(bias_rows, model)
    vectors = jnp.concatenate(
        [
            jnp.zeros((2, model), jnp.float32),
            jnp.sum(cot_rows, axis=0)[None],
            jnp.zeros((5, model), jnp.float32),
            biases,
            jnp.zeros((-bias_rows % 8, model), jnp.float32),
        ]
    )
    up_grad, down_grad, qkv_grad, out_grad, branch, row_grad, sums = scatter_all(
        grads,
        branch.astype(jnp.bfloat16),
        feature_grad.astype(jnp.bfloat16),
        normed,
        vectors,
    )
    layer_output = (own_rows + branch + out_bias + down_bias).astype(jnp.bfloat16)
    gain_grad, shift_grad, bias_grad = sums[0], sums[1], sums[2]
    bias_flat = sums[8 : 8 + bias_rows].reshape(-1)
    qkv_bias_grad = bias_flat[:width_qkv]
    up_bias_grad = bias_flat[width_qkv : width_qkv + width_up]
    scaled = row_grad * norm_gain
    input_grad = (
        cot_rows
        + inverse
        * (
            scaled
            - jnp.mean(scaled, axis=-1, keepdims=True)
            - normed * jnp.mean(scaled * normed, axis=-1, keepdims=True)
        )
    ).astype(jnp.bfloat16)
    return (
        layer_output,
        input_grad,
        gain_grad,
        shift_grad,
        qkv_grad,
        qkv_bias_grad,
        out_grad.T,
        bias_grad,
        up_grad,
        up_bias_grad,
        down_grad.T,
        bias_grad,
    )


DOCS = 4


def error_function(value):
    x = jnp.clip(value, -3.7439211627767994, 3.7439211627767994)
    y = x * x
    top = jnp.float32(0.00022905065861350646)
    for c in (
        0.0034082910107109506,
        0.050955695062380861,
        0.18520832239976145,
        1.128379143519084,
    ):
        top = top * y + jnp.float32(c)
    low = jnp.float32(-1.1791602954361697e-7)
    for c in (
        0.000023547966471313185,
        0.0010179625278914885,
        0.014070470171167667,
        0.11098505178285362,
        0.49746925110067538,
        1.0,
    ):
        low = low * y + jnp.float32(c)
    return x * top / low


def layer_kernel(
    fsdp,
    tp,
    heads,
    x_ref,
    c_ref,
    seg_ref,
    gain_ref,
    shift_ref,
    ob_ref,
    db_ref,
    bq_ref,
    bu_ref,
    wq_ref,
    wo_ref,
    wu_ref,
    wd_ref,
    y_out,
    dx_out,
    gq_out,
    go_out,
    gu_out,
    gd_out,
    v_out,
    w_all,
    h_all,
    c_all,
    h_turn,
    c_turn,
    normed_ref,
    inverse_ref,
    cos_ref,
    sin_a,
    sin_b,
    start_ref,
    qkv_ref,
    do_ref,
    queries,
    keys_in,
    values_in,
    grads_in,
    mixed,
    grad_q,
    grad_k,
    grad_v,
    o_ref,
    packed,
    gelu_ref,
    pre_ref,
    g_all,
    halves,
    joined,
    lands,
    part,
    mates,
    summed,
    sides_in,
    d_out,
    early,
    early_all,
    rows,
    rows_all,
    shared,
    up_send,
    down_send,
    far_send,
    z_recv,
    y_send,
    y_recv,
    x_send,
    x_recv,
    m_send,
    m_recv,
    a_send,
    a_recv,
    l_send,
    l_recv,
    pm_send,
    pm_recv,
    px_send,
    px_recv,
    e_send,
    e_recv,
    v_send,
    v_recv,
    u_send,
    u_recv,
):
    f32 = jnp.float32
    bf16 = jnp.bfloat16
    f, t, pair, line = place(fsdp, tp)
    lines = fsdp // 2
    sides = tp // 2
    side = lax.div(t, 2)
    par = lax.rem(t, 2)
    partner = 2 * line + 1 - pair
    mate = 2 * side + 1 - par
    block = x_ref.shape[0]
    model = x_ref.shape[1]
    shard = wu_ref.shape[0]
    hidden = wu_ref.shape[1]
    wide = wq_ref.shape[1]
    length = tp * block
    two = 2 * HEAD_DIM
    scale = HEAD_DIM ** (-0.5)
    half = ROT // 2

    barrier = pltpu.get_barrier_semaphore()
    each(
        1,
        fsdp,
        lambda step: pl.semaphore_signal(
            barrier, inc=1, device_id=(lax.rem(f + step, fsdp), t), device_id_type=MESH
        ),
    )
    each(
        1,
        tp,
        lambda step: pl.semaphore_signal(
            barrier, inc=1, device_id=(f, lax.rem(t + step, tp)), device_id_type=MESH
        ),
    )
    w_all[0, f] = jnp.concatenate([wq_ref[...], wo_ref[...].T], axis=1)
    w_all[1, f] = wu_ref[...]
    w_all[2, f] = wd_ref[...]
    c_all[t] = c_ref[...]
    own = x_ref[...].astype(f32)
    normed, inverse, shifted = layer_norm(own, gain_ref[...][None], shift_ref[...][None])
    h_all[t] = shifted.astype(bf16)
    normed_ref[...] = normed
    inverse_ref[...] = inverse
    pl.semaphore_wait(barrier, fsdp + tp - 2)

    def slot(origin):
        return 2 * origin + pair

    def z_copy(i, origin, send, to):
        view = w_all.at[i, slot(origin)]
        return remote(view, view, send.at[i, origin], z_recv.at[i, origin], (2 * to + pair, t))

    def z_up(i, origin):
        return z_copy(i, origin, up_send, line + 1)

    def z_down(i, origin):
        return z_copy(i, origin, down_send, line - 1)

    last_line = lines - 1
    direct = lines > 2

    def far(i):
        view = w_all.at[i, f]
        return remote(
            view,
            view,
            far_send.at[i],
            z_recv.at[i, line],
            (2 * (last_line - line) + pair, t),
        )

    def at_end():
        return (line == 0) | (line == last_line)

    def y_copy(i, origin, side_of):
        view = w_all.at[i, 2 * origin + side_of]
        return remote(view, view, y_send.at[i, origin], y_recv.at[i, origin], (partner, t))

    def send_own(i):
        @pl.when(line + 1 < lines)
        def _():
            z_up(i, line).start()

        @pl.when(line > 0)
        def _():
            z_down(i, line).start()

        y_copy(i, line, pair).start()
        if direct:

            @pl.when(at_end())
            def _():
                far(i).start()

    def relay(r):
        i = lax.div(r, lines - 1)
        k = lax.rem(r, lines - 1) + 1
        below = line - k
        above = line + k

        @pl.when(below >= 0)
        def _():
            z_up(i, below).wait_recv()

            @pl.when((line + 1 < lines) & (not direct or (line + 1 - below < last_line)))
            def _():
                z_up(i, below).start()

            y_copy(i, below, pair).start()

        @pl.when(above < lines)
        def _():
            z_down(i, above).wait_recv()

            @pl.when((line > 0) & (not direct or (above - line + 1 < last_line)))
            def _():
                z_down(i, above).start()

            y_copy(i, above, pair).start()

    relays = 3 * (lines - 1)

    tokens = (h_all, c_all)

    def x_copy(which, step, place_of):
        view = tokens[which].at[place_of]
        other = lax.rem(side + step, sides)
        return remote(
            view, view, x_send.at[which, step], x_recv.at[which, step], (f, 2 * other + par)
        )

    def m_copy(which, origin, parity):
        view = tokens[which].at[2 * origin + parity]
        return remote(
            view, view, m_send.at[which, origin], m_recv.at[which, origin], (f, mate)
        )

    def arrive(which):
        def one(step):
            origin = lax.rem(side + sides - step, sides)
            x_copy(which, step, 2 * origin + par).wait_recv()
            m_copy(which, origin, par).start()

        each(1, sides, one)

    def settle(which):
        each(0, sides, lambda origin: m_copy(which, origin, 1 - par).wait_recv())

    each(1, sides, lambda step: x_copy(0, step, t).start())
    send_own(0)
    m_copy(0, side, par).start()
    each(1, sides, lambda step: x_copy(1, step, t).start())
    m_copy(1, side, par).start()
    send_own(1)

    seg = seg_ref[...]
    down_rows = lax.broadcasted_iota(jnp.int32, (length, 1), 0)
    along_row = lax.broadcasted_iota(jnp.int32, (1, length), 1)
    start_col = jnp.zeros((length, 1), jnp.int32)
    start_row = jnp.zeros((1, length), jnp.int32)
    for d in range(1, DOCS):
        count = jnp.sum((seg < d).astype(jnp.int32), axis=1, keepdims=True)
        start_col = jnp.where(down_rows >= count, count, start_col)
        start_row = jnp.where(along_row >= count, count, start_row)
    start_ref[...] = start_col
    spot = (along_row - start_row).astype(f32)
    order = lax.broadcasted_iota(jnp.int32, (half, 1), 0).astype(f32)
    rates = jnp.exp(order * (-2.0 / ROT * 9.210340371976184))
    angles = spot * rates
    lane = lax.broadcasted_iota(jnp.int32, (half, two), 1) % HEAD_DIM
    pick = lax.broadcasted_iota(jnp.int32, (half, two), 0)
    first_half = (lane == pick).astype(f32)
    last_half = (lane == pick + half).astype(f32)

    def spread_out(table, matrix):
        return lax.dot_general(
            table,
            matrix,
            (((0,), (0,)), ((), ())),
            precision=lax.Precision.HIGHEST,
            preferred_element_type=f32,
        )

    cosine = jnp.cos(angles)
    sine = jnp.sin(angles)
    beyond = lax.broadcasted_iota(jnp.int32, (1, two), 1) % HEAD_DIM >= ROT
    cos_ref[...] = jnp.where(beyond, 1.0, spread_out(cosine, first_half + last_half))
    sin_a[...] = spread_out(sine, last_half)
    sin_b[...] = -spread_out(sine, first_half)

    each(0, lines - 1, relay)
    send_own(2)
    arrive(0)
    ahead_of = (lines - 1) + min(2, lines - 1)
    relay(lines - 1)
    settle(0)
    for s in range(tp):
        h_turn[:, s * block : (s + 1) * block] = h_all[s].T
    each(lines, ahead_of, relay)
    each(0, lines, lambda origin: y_copy(0, origin, 1 - pair).wait_recv())

    def project_q(s, carry):
        weight = w_all[0].reshape(model, model)
        part_of = pl.ds(s * block, block)
        qkv_ref[part_of] = (
            jnp.dot(h_all[s], weight[:, :wide], preferred_element_type=f32) + bq_ref[...][None]
        )
        return carry

    lax.fori_loop(0, tp, project_q, 0)
    arrive(1)

    def rotated(value, spots, sign):
        return (
            value * cos_ref[spots]
            + sign
            * (
                pltpu.roll(value, half, 1) * sin_a[spots]
                + pltpu.roll(value, two - half, 1) * sin_b[spots]
            )
        )

    for n in range(heads):
        base = 3 * HEAD_DIM * n

        def prepare(s, carry, n=n, base=base):
            spots = pl.ds(s * block, block)
            both = rotated(qkv_ref[spots, base : base + two], spots, 1.0)
            queries[n, spots] = both[:, :HEAD_DIM].astype(bf16) * bf16(scale)
            keys_in[n, spots] = both[:, HEAD_DIM:].astype(bf16)
            values_in[n, spots] = qkv_ref[spots, base + two : base + two + HEAD_DIM].astype(bf16)
            return carry

        lax.fori_loop(0, tp, prepare, 0)
    settle(1)
    for s in range(tp):
        c_turn[:, s * block : (s + 1) * block] = c_all[s].T

    def project_o(s, carry):
        weight = w_all[0].reshape(model, model)
        spots = pl.ds(s * block, block)
        value = jnp.dot(c_all[s], weight[:, wide:], preferred_element_type=f32).astype(bf16)
        for n in range(heads):
            grads_in[n, spots] = value[:, n * HEAD_DIM : (n + 1) * HEAD_DIM]
        return carry

    lax.fori_loop(0, tp, project_o, 0)
    grad_k[...] = jnp.zeros_like(grad_k)
    grad_v[...] = jnp.zeros_like(grad_v)
    span = min(SPAN, length)
    parts = length // span
    steps = heads * parts
    busy = max(1, steps * 3 // 4)
    left = relays - ahead_of

    def due(j):
        return ahead_of + jnp.minimum(left, lax.div(j * left, busy))

    def one_head(n, carry):
        for m in range(parts):
            first = m * span
            last = first + span
            low = max(0, (first - MOST) // span * span)
            spots = slice(first, last)
            window = slice(low, last)
            q = queries[n, spots]
            k = keys_in[n, window]
            v = values_in[n, window]
            g = grads_in[n, spots]
            shape = (span, last - low)
            key_at = lax.broadcasted_iota(jnp.int32, shape, 1) + low
            allowed = (key_at >= start_ref[spots]) & (
                lax.broadcasted_iota(jnp.int32, shape, 0) + first >= key_at
            )
            scores = jnp.where(allowed, cross_cols(q, k), -1e30)
            exps = jnp.exp(scores - jnp.max(scores, axis=-1, keepdims=True))
            probs = exps * (1.0 / jnp.sum(exps, axis=-1, keepdims=True))
            weights = probs.astype(bf16)
            out = jnp.dot(weights, v, preferred_element_type=f32).astype(bf16)
            mixed[n, spots] = out
            delta = jnp.sum(g.astype(f32) * out.astype(f32), axis=-1, keepdims=True)
            grad_probs = cross_cols(g, v)
            grad_scores = (probs * (grad_probs - delta)).astype(bf16)
            grad_q[n, spots] = jnp.dot(grad_scores, k, preferred_element_type=f32) * scale
            grad_k[n, window] += cross_rows(grad_scores, q)
            grad_v[n, window] += cross_rows(weights, g)
            j = n * parts + m
            each(due(j), due(j + 1), relay)
        return carry

    lax.fori_loop(0, heads, one_head, 0)

    early[...] = jnp.zeros_like(early)

    def finish(s, carry):
        spots = pl.ds(s * block, block)
        pieces = []
        for n in range(heads):
            both = jnp.concatenate([grad_q[n, spots], grad_k[n, spots]], axis=1)
            pieces += [rotated(both, spots, -1.0), grad_v[n, spots]]
        whole = jnp.concatenate(pieces, axis=1)
        early[0:1, :wide] += jnp.sum(whole, axis=0, keepdims=True)
        packed[spots] = whole.astype(bf16)
        o_ref[spots] = jnp.concatenate([mixed[n, spots] for n in range(heads)], axis=1)
        return carry

    lax.fori_loop(0, tp, finish, 0)

    def ahead(step):
        return lax.rem(line + step, lines)

    def across(i, step):
        return remote(
            g_all.at[i, 2 * ahead(step) + 1 - pair],
            halves.at[i, step],
            a_send.at[i, step],
            a_recv.at[i, step],
            (partner, t),
        )

    def along(i, step):
        return remote(
            joined.at[i, step],
            lands.at[i, step],
            l_send.at[i, step],
            l_recv.at[i, step],
            (2 * ahead(step) + pair, t),
        )

    def start_across(i):
        each(1, lines, lambda step: across(i, step).start())
        across(i, 0).start()

    def join(i, step):
        across(i, step).wait_recv()
        joined[i, step] = (
            g_all[i, 2 * ahead(step) + pair].astype(f32) + halves[i, step].astype(f32)
        ).astype(bf16)
        along(i, step).start()

    tile = model // 2
    many = tile // shard

    def store_grad(i, j, value):
        g_all[i, pl.ds(j * many, many)] = value.astype(bf16).reshape(many, shard, value.shape[1])

    def grad_attention(j, carry):
        spots = pl.ds(j * tile, tile)
        store_grad(
            0,
            j,
            jnp.concatenate(
                [
                    jnp.dot(h_turn[spots], packed[...], preferred_element_type=f32),
                    jnp.dot(c_turn[spots], o_ref[...], preferred_element_type=f32),
                ],
                axis=1,
            ),
        )
        return carry

    def grad_up(j, carry):
        store_grad(
            1,
            j,
            jnp.dot(h_turn[pl.ds(j * tile, tile)], pre_ref[...], preferred_element_type=f32),
        )
        return carry

    def grad_down(j, carry):
        store_grad(
            2,
            j,
            jnp.dot(c_turn[pl.ds(j * tile, tile)], gelu_ref[...], preferred_element_type=f32),
        )
        return carry

    lax.fori_loop(0, 2, grad_attention, 0)
    start_across(0)

    each(due(steps), relays, relay)
    each(0, lines, lambda origin: y_copy(1, origin, 1 - pair).wait_recv())
    each(0, lines, lambda origin: y_copy(2, origin, 1 - pair).wait_recv())

    def hidden_rows(s, carry):
        spots = pl.ds(s * block, block)
        up = w_all[1].reshape(model, hidden)
        down = w_all[2].reshape(model, hidden)
        a = jnp.dot(h_all[s], up, preferred_element_type=f32) + bu_ref[...][None]
        bell = 0.5 * (1.0 + error_function(a * 0.7071067811865476))
        gelu_ref[spots] = (a * bell).astype(bf16)
        slope = bell + a * jnp.exp(-0.5 * a * a) * 0.3989422804014327
        grad = jnp.dot(c_all[s], down, preferred_element_type=f32) * slope
        early[1:2, :hidden] += jnp.sum(grad, axis=0, keepdims=True)
        pre_ref[spots] = grad.astype(bf16)
        return carry

    lax.fori_loop(0, tp, hidden_rows, 0)

    def e_copy(step, place_of):
        return remote(
            early,
            early_all.at[place_of],
            e_send.at[step],
            e_recv.at[step],
            (lax.rem(f + step, fsdp), t),
        )

    early[2:3] = jnp.sum(c_all[t].astype(f32), axis=0, keepdims=True)
    join(0, 1)
    lax.fori_loop(0, 2, grad_up, 0)
    start_across(1)
    each(1, fsdp, lambda step: e_copy(step, f).start())
    join(0, 2)

    def pm_copy(which, origin):
        return remote(
            part.at[which, 2 * origin + 1 - par],
            mates.at[which, origin],
            pm_send.at[which, origin],
            pm_recv.at[which, origin],
            (f, mate),
        )

    def px_copy(which, step):
        other = lax.rem(side + step, sides)
        return remote(
            summed.at[which, step],
            sides_in.at[which, step],
            px_send.at[which, step],
            px_recv.at[which, step],
            (f, 2 * other + par),
        )

    def feature_rows(s, carry):
        spots = pl.ds(s * block, block)
        weight = w_all[0].reshape(model, model)
        part[0, s] = (
            cross_cols(packed[spots], weight[:, :wide])
            + cross_cols(pre_ref[spots], w_all[1].reshape(model, hidden))
        ).astype(bf16)
        return carry

    def branch_rows(s, carry):
        spots = pl.ds(s * block, block)
        weight = w_all[0].reshape(model, model)
        part[1, s] = (
            cross_cols(o_ref[spots], weight[:, wide:])
            + cross_cols(gelu_ref[spots], w_all[2].reshape(model, hidden))
        ).astype(bf16)
        return carry

    def pass_on(which):
        def one(step):
            other = lax.rem(side + step, sides)
            pm_copy(which, other).wait_recv()
            summed[which, step] = (
                part[which, 2 * other + par].astype(f32) + mates[which, other].astype(f32)
            ).astype(bf16)
            px_copy(which, step).start()

        each(1, sides, one)

    def gathered(which):
        pm_copy(which, side).wait_recv()
        d_out[...] = part[which, t].astype(f32) + mates[which, side].astype(f32)

        def one(step):
            px_copy(which, step).wait_recv()
            d_out[...] += sides_in[which, step].astype(f32)

        each(1, sides, one)

    lax.fori_loop(0, tp, feature_rows, 0)
    each(0, sides, lambda origin: pm_copy(0, origin).start())
    each(3, lines, lambda step: join(0, step))
    lax.fori_loop(0, 2, grad_down, 0)
    start_across(2)
    pass_on(0)
    lax.fori_loop(0, tp, branch_rows, 0)
    each(0, sides, lambda origin: pm_copy(1, origin).start())
    join(1, 1)
    pass_on(1)
    each(2, lines, lambda step: join(1, step))

    gathered(0)
    rows[...] = jnp.zeros_like(rows)
    rows[0:1] = jnp.sum(d_out[...] * normed_ref[...], axis=0, keepdims=True)
    rows[1:2] = jnp.sum(d_out[...], axis=0, keepdims=True)
    rows[2:3] = early[2:3]

    def v_copy(step, place_of):
        return remote(
            rows,
            rows_all.at[place_of],
            v_send.at[step],
            v_recv.at[step],
            (lax.rem(f + step, fsdp), t),
        )

    each(1, fsdp, lambda step: v_copy(step, f).start())
    rows_all[f] = rows[...]
    normed = normed_ref[...]
    scaled = d_out[...] * gain_ref[...][None]
    dx_out[...] = (
        c_ref[...].astype(f32)
        + inverse_ref[...]
        * (
            scaled
            - jnp.mean(scaled, axis=-1, keepdims=True)
            - normed * jnp.mean(scaled * normed, axis=-1, keepdims=True)
        )
    ).astype(bf16)
    each(1, lines - 1, lambda step: join(2, step))
    gathered(1)
    y_out[...] = (
        x_ref[...].astype(f32) + d_out[...] + ob_ref[...][None] + db_ref[...][None]
    ).astype(bf16)
    each(lines - 1, lines, lambda step: join(2, step))
    each(1, fsdp, lambda step: e_copy(step, lax.rem(f + fsdp - step, fsdp)).wait_recv())
    early_all[f] = early[...]
    total = lax.fori_loop(1, fsdp, lambda step, value: value + early_all[step], early_all[0])
    v_out[8:16] = total
    each(1, fsdp, lambda step: v_copy(step, lax.rem(f + fsdp - step, fsdp)).wait_recv())
    shared[t] = lax.fori_loop(1, fsdp, lambda step, value: value + rows_all[step], rows_all[0])

    def u_copy(step, place_of):
        view = shared.at[place_of]
        return remote(
            shared.at[t],
            view,
            u_send.at[step],
            u_recv.at[step],
            (f, lax.rem(t + step, tp)),
        )

    each(1, tp, lambda step: u_copy(step, t).start())
    def collected(i):
        across(i, 0).wait_recv()
        value = g_all[i, f].astype(f32) + halves[i, 0].astype(f32)

        def one(step, value):
            along(i, step).wait_recv()
            return value + lands[i, step].astype(f32)

        return lax.fori_loop(1, lines, one, value)

    value = collected(0)
    gq_out[...] = value[:, :wide]
    go_out[...] = value[:, wide:]
    gu_out[...] = collected(1)
    gd_out[...] = collected(2)

    each(1, tp, lambda step: u_copy(step, lax.rem(t + tp - step, tp)).wait_recv())
    whole = shared[0]
    for step in range(1, tp):
        whole = whole + shared[step]
    v_out[0:8] = whole

    for i in range(3):

        @pl.when(line + 1 < lines)
        def _():
            first = jnp.maximum(0, line + 2 - last_line) if direct else 0
            each(first, line + 1, lambda origin: z_up(i, origin).wait_send())

        @pl.when(line > 0)
        def _():
            end = jnp.minimum(lines, line + last_line - 1) if direct else lines
            each(line, end, lambda origin: z_down(i, origin).wait_send())

        if direct:

            @pl.when(at_end())
            def _():
                far(i).wait_send()

        each(0, lines, lambda origin: y_copy(i, origin, pair).wait_send())
        each(0, lines, lambda step: across(i, step).wait_send())
        each(1, lines, lambda step: along(i, step).wait_send())
    for which in range(2):
        each(1, sides, lambda step: x_copy(which, step, t).wait_send())
        each(0, sides, lambda origin: m_copy(which, origin, par).wait_send())
        each(0, sides, lambda origin: pm_copy(which, origin).wait_send())
        each(1, sides, lambda step: px_copy(which, step).wait_send())
    each(1, fsdp, lambda step: e_copy(step, f).wait_send())
    each(1, fsdp, lambda step: v_copy(step, f).wait_send())
    each(1, tp, lambda step: u_copy(step, t).wait_send())


def layer_call(x, c, seg, gain, shift, ob, db, bq, bu, wq, wo, wu, wd):
    fsdp = lax.axis_size("fsdp")
    tp = lax.axis_size("tp")
    lines = fsdp // 2
    sides = tp // 2
    block, model = x.shape
    shard, hidden = wu.shape
    wide = wq.shape[1]
    heads = wide // (3 * HEAD_DIM)
    length = tp * block
    two = 2 * HEAD_DIM
    f32 = jnp.float32
    bf16 = jnp.bfloat16
    vmem = pl.BlockSpec(memory_space=pltpu.VMEM)
    dma = pltpu.SemaphoreType.DMA
    buf = pltpu.VMEM
    return pl.pallas_call(
        functools.partial(layer_kernel, fsdp, tp, heads),
        out_shape=(
            jax.ShapeDtypeStruct((block, model), bf16),
            jax.ShapeDtypeStruct((block, model), bf16),
            jax.ShapeDtypeStruct((shard, wide), f32),
            jax.ShapeDtypeStruct((shard, model - wide), f32),
            jax.ShapeDtypeStruct((shard, hidden), f32),
            jax.ShapeDtypeStruct((shard, hidden), f32),
            jax.ShapeDtypeStruct((16, model), f32),
        ),
        in_specs=[vmem] * 13,
        out_specs=(vmem,) * 7,
        scratch_shapes=[
            buf((3, fsdp, shard, model), bf16),
            buf((tp, block, model), bf16),
            buf((tp, block, model), bf16),
            buf((model, length), bf16),
            buf((model, length), bf16),
            buf((block, model), f32),
            buf((block, 1), f32),
            buf((length, two), f32),
            buf((length, two), f32),
            buf((length, two), f32),
            buf((length, 1), jnp.int32),
            buf((length, wide), f32),
            buf((8, 128), f32),
        ]
        + [buf((heads, length, HEAD_DIM), bf16)] * 5
        + [buf((heads, length, HEAD_DIM), f32)] * 3
        + [
            buf((length, heads * HEAD_DIM), bf16),
            buf((length, wide), bf16),
            buf((length, hidden), bf16),
            buf((length, hidden), bf16),
            buf((3, fsdp, shard, model), bf16),
            buf((3, lines, shard, model), bf16),
            buf((3, lines, shard, model), bf16),
            buf((3, lines, shard, model), bf16),
            buf((2, tp, block, model), bf16),
            buf((2, sides, block, model), bf16),
            buf((2, sides, block, model), bf16),
            buf((2, sides, block, model), bf16),
            buf((block, model), f32),
            buf((8, model), f32),
            buf((fsdp, 8, model), f32),
            buf((8, model), f32),
            buf((fsdp, 8, model), f32),
            buf((tp, 8, model), f32),
        ]
        + [dma((3, lines))] * 2
        + [dma((3,))]
        + [dma((3, lines))] * 3
        + [dma((2, sides))] * 4
        + [dma((3, lines))] * 4
        + [dma((2, sides))] * 4
        + [dma((fsdp,))] * 4
        + [dma((tp,))] * 2,
        compiler_params=pltpu.CompilerParams(
            collective_id=3, has_side_effects=True, vmem_limit_bytes=62 * 1024 * 1024
        ),
        name="layer",
    )(x, c, seg, gain, shift, ob, db, bq, bu, wq, wo, wu, wd)


def deliver_kernel(y, dx, gq, go, gu, gd, v, *refs):
    outs, (turned, sums, sems) = refs[:12], refs[12:]
    pairs = (
        (v, sums),
        (go, turned),
        (y, outs[0]),
        (dx, outs[1]),
        (gq, outs[4]),
        (gu, outs[8]),
        (gd, outs[10]),
    )
    copies = [
        pltpu.make_async_copy(source, target, sems.at[i])
        for i, (source, target) in enumerate(pairs)
    ]
    for copy in copies:
        copy.start()
    copies[0].wait()
    for place_of, row in ((2, 0), (3, 1), (5, 8), (7, 2), (9, 9), (11, 2)):
        outs[place_of][...] = sums[row][: outs[place_of].shape[0]]
    copies[1].wait()
    outs[6][...] = turned[...].T
    for copy in copies[2:]:
        copy.wait()


def deliver(y, dx, gq, go, gu, gd, v):
    f32 = jnp.float32
    vmem = pl.BlockSpec(memory_space=pltpu.VMEM)
    line = jax.ShapeDtypeStruct((y.shape[1],), f32)
    return pl.pallas_call(
        deliver_kernel,
        out_shape=(
            jax.ShapeDtypeStruct(y.shape, y.dtype),
            jax.ShapeDtypeStruct(dx.shape, dx.dtype),
            line,
            line,
            jax.ShapeDtypeStruct(gq.shape, f32),
            jax.ShapeDtypeStruct((gq.shape[1],), f32),
            jax.ShapeDtypeStruct((go.shape[1], go.shape[0]), f32),
            line,
            jax.ShapeDtypeStruct(gu.shape, f32),
            jax.ShapeDtypeStruct((gu.shape[1],), f32),
            jax.ShapeDtypeStruct(gd.shape, f32),
            line,
        ),
        in_specs=[pl.BlockSpec(memory_space=pl.ANY)] * 7,
        out_specs=(vmem,) * 12,
        scratch_shapes=[
            pltpu.VMEM(go.shape, f32),
            pltpu.VMEM(v.shape, f32),
            pltpu.SemaphoreType.DMA((7,)),
        ],
        compiler_params=pltpu.CompilerParams(vmem_limit_bytes=60 * 1024 * 1024),
        name="deliver",
    )(y, dx, gq, go, gu, gd, v)


def fused_body(
    layer_input,
    out_cotangent,
    segments,
    norm_gain,
    norm_bias,
    qkv_weight,
    qkv_bias,
    out_weight,
    out_bias,
    up_weight,
    up_bias,
    down_weight,
    down_bias,
):
    y, dx, qkv_grad, out_grad, up_grad, down_grad, sums = layer_call(
        layer_input,
        out_cotangent,
        segments,
        norm_gain,
        norm_bias,
        out_bias,
        down_bias,
        qkv_bias,
        up_bias,
        qkv_weight,
        out_weight,
        up_weight,
        down_weight.T,
    )
    outs = list(deliver(y, dx, qkv_grad, out_grad, up_grad, down_grad, sums))
    outs[10] = outs[10].T
    return tuple(outs)


def body(*args):
    rows = args[5].shape[0]
    model, hidden = args[9].shape[0] * lax.axis_size("fsdp"), args[9].shape[1]
    fits = (
        rows % 16 == 0
        and (model // 2) % rows == 0
        and args[5].shape[1] + args[7].shape[0] == model == hidden
        and args[2].shape == (1, lax.axis_size("tp") * args[0].shape[0])
        and args[0].shape[0] == SPAN
    )
    return fused_body(*args) if fits else staged_body(*args)


def solution(mesh):
    in_specs = (
        P(("fsdp", "tp"), None),
        P(("fsdp", "tp"), None),
        P("fsdp", None),
        P(),
        P(),
        P("fsdp", "tp"),
        P("tp"),
        P("tp", "fsdp"),
        P(),
        P("fsdp", "tp"),
        P("tp"),
        P("tp", "fsdp"),
        P(),
    )
    out_specs = (
        P(("fsdp", "tp"), None),
        P(("fsdp", "tp"), None),
        P(),
        P(),
        P("fsdp", "tp"),
        P("tp"),
        P("tp", "fsdp"),
        P(),
        P("fsdp", "tp"),
        P("tp"),
        P("tp", "fsdp"),
        P(),
    )
    return jax.shard_map(body, mesh=mesh, in_specs=in_specs, out_specs=out_specs, check_vma=False)
```
